256 devices in a mesh: dp: 4 (over z_hi, core), expert: 64 (over x, y, z_lo).
Axes of the slice: x: 4, y: 4, z: 8 (z_hi: 2, z_lo: 4; z = z_hi * 4 + z_lo), core: 2. Of those that a mesh axis runs over, the one named last changes fastest.
Arguments:
- query: bfloat16 [2, 16384, 2560], P(None, ('dp', 'expert')), may hold values from -24 to 24
- keys: bfloat16 [2, 16384, 512], P(None, ('dp', 'expert')), may hold values from -4 to 4
- values: bfloat16 [2, 16384, 512], P(None, ('dp', 'expert')), may hold values from -6 to 6
- lengths: int32 [2, 256, 4], P(None, ('dp', 'expert')), may hold values from 0 to 64, as said below
- routes: int32 [2, 16384, 6], P(None, ('dp', 'expert')), may hold values from 0 to 63, as said below
- gates: float32 [2, 16384, 6], P(None, ('dp', 'expert')), may hold values from 0.05 to 0.4
- norm_gain: float32 [2560], replicated, may hold values from 0.1 to 1.9
- old_holds: int32 [64], replicated, may hold values from 0 to 63, as said below
- dup_experts: int32 [4], replicated, may hold values from 0 to 63, as said below
- w_gate: bfloat16 [64, 2560, 768], P('expert'), may hold values from -0.125 to 0.125
- w_up: bfloat16 [64, 2560, 768], P('expert'), may hold values from -0.125 to 0.125
- w_down: bfloat16 [64, 768, 2560], P('expert'), may hold values from -0.21875 to 0.21875
Outputs:
- layer_out: bfloat16 [2, 16384, 2560], P(None, ('dp', 'expert'))
The draws below stay inside these ranges and needn't reach their ends.
Inputs may be any that keep to these rules, and one draw needn't show every extreme that they name: Each length is a multiple of 8; the 4 lengths of one device in one batch add up to 64. `routes`: each token names 6 different experts. `dup_experts`: 4 different experts. `old_holds`: each expert stands in exactly one slot.
All inputs are finite; a program needn't handle non-finite values.
Results may differ from the reference program's by a relative error of at most 0.0061.
Values may be sent and summed in bfloat16 or wider, within the bound.
A program may use at most 128 MiB of HBM per device.

```python
import jax
import jax.numpy as jnp
from jax import lax

D = 2560
QUERY_HEAD_COUNT = 20
SHARED_KV_HEADS = 4
HEAD_WIDTH = 128
TOPK = 6
FFW = 768
NDUP = 4
REQ = 4
TOK = 64
EXPERTS = 64
BATCH_TOKENS = 16384
CAP = 6


def drawn_pair(key):
    base_query = jax.random.fold_in(key, 101)
    base_keys = jax.random.fold_in(key, 102)
    query_shape = (2, BATCH_TOKENS, QUERY_HEAD_COUNT * HEAD_WIDTH)
    key_layout = (2, BATCH_TOKENS, SHARED_KV_HEADS * HEAD_WIDTH)
    query = jnp.clip(jax.random.normal(base_query, query_shape, jnp.float32), -4.0, 4.0)
    keys = jnp.clip(jax.random.normal(base_keys, key_layout, jnp.float32), -4.0, 4.0)
    return (query.astype(jnp.bfloat16), keys.astype(jnp.bfloat16))


def draw_query(key, part):
    return drawn_pair(key)[0]


def draw_keys(key, part):
    return drawn_pair(key)[1]


def draw_lengths(key, part):
    units = TOK // 8
    count = BATCH_TOKENS // TOK
    cuts = jax.random.randint(jax.random.fold_in(key, 301), (2, count, REQ - 1), 0, units + 1)
    cuts = jnp.sort(cuts, axis=-1)
    device = lax.iota(jnp.int32, count)
    cuts = jnp.where((device == 0)[None, :, None], units, cuts)
    edges = jnp.concatenate([jnp.zeros((2, count, 1), jnp.int32), cuts.astype(jnp.int32), jnp.full((2, count, 1), units, jnp.int32)], axis=-1)
    return ((edges[..., 1:] - edges[..., :-1]) * 8).astype(jnp.int32)


def slot_order(key):
    return jax.random.permutation(jax.random.fold_in(key, 201), EXPERTS).astype(jnp.int32)


def hot_set(key):
    order = slot_order(key)
    middle = EXPERTS // 2
    chosen_slots = jnp.array([0, middle - 1, middle, EXPERTS - 1], jnp.int32)
    hot = order[chosen_slots].astype(jnp.int32)
    present = jnp.sum((hot == EXPERTS - 1).astype(jnp.int32)) > 0
    last_pick = jnp.where(present, hot[3], EXPERTS - 1).astype(jnp.int32)
    return hot.at[3].set(last_pick).astype(jnp.int32)


def draw_old_holds(key, part):
    return slot_order(key)


def draw_routes(key, part):
    hot = hot_set(key)
    expert_list = lax.iota(jnp.int32, EXPERTS)
    router_logits = jax.random.randint(jax.random.fold_in(key, 202), (2, BATCH_TOKENS, EXPERTS), 0, 2 ** 20) * EXPERTS
    router_logits = router_logits + expert_list[None, None, :]
    selected_experts = hot[lax.iota(jnp.int32, BATCH_TOKENS) % NDUP]
    extra_reward = (selected_experts[:, None] == expert_list[None, :]).astype(jnp.int32) * 2 ** 27
    router_logits = router_logits + extra_reward[None]
    _, picked = lax.top_k(router_logits, TOPK)
    return picked.astype(jnp.int32)


def draw_dup_experts(key, part):
    return hot_set(key)


def block_scale(key, dims, shards, smallest, largest):
    level = 1.0
    for axis_at, blocks in shards:
        steps = jax.random.uniform(jax.random.fold_in(jax.random.fold_in(key, 6), axis_at), (blocks,), jnp.float32, smallest / len(shards), largest / len(shards))
        level = level * jnp.repeat(jnp.exp(steps), dims[axis_at] // blocks).reshape((-1,) + (1,) * (len(dims) - 1 - axis_at))
    return level


def gaussian(rng, dims, scale, reach, cuts=(), kind=jnp.bfloat16):
    level = block_scale(rng, dims, cuts, -0.22, 0.18) if cuts else 1.0
    values = jax.random.normal(rng, dims, jnp.float32) * scale * level
    return jnp.minimum(jnp.maximum(values, -reach), reach).astype(kind)


def setup_inputs(seed: int = 0) -> dict:
    key_of = jax.random.split(jax.random.key(seed), 13)
    query = draw_query(jax.random.fold_in(key_of[12], 71), 0)
    keys = draw_keys(jax.random.fold_in(key_of[12], 71), 0)
    values = gaussian(key_of[2], (2, BATCH_TOKENS, SHARED_KV_HEADS * HEAD_WIDTH), 1.0, 6.0, ((1, 256),))
    lengths = draw_lengths(jax.random.fold_in(key_of[12], 71), 0)
    routes = draw_routes(jax.random.fold_in(key_of[12], 71), 0)
    gates = jnp.clip(0.05 + 0.35 * jax.random.uniform(key_of[5], (2, BATCH_TOKENS, TOPK), jnp.float32) ** block_scale(key_of[5], (2, BATCH_TOKENS, TOPK), ((1, 256),), -0.2, 0.2), 0.05, 0.4)
    norm_gain = jnp.clip(1.0 + 0.18 * jax.random.normal(key_of[6], (D,), jnp.float32), 0.1, 1.9)
    old_holds = draw_old_holds(jax.random.fold_in(key_of[12], 71), 0)
    dup_experts = draw_dup_experts(jax.random.fold_in(key_of[12], 71), 0)
    w_gate = gaussian(key_of[9], (EXPERTS, D, FFW), D ** -0.5, 0.125, ((0, 64),))
    w_up = gaussian(key_of[10], (EXPERTS, D, FFW), D ** -0.5, 0.125, ((0, 64),))
    w_down = gaussian(key_of[11], (EXPERTS, FFW, D), FFW ** -0.5, 0.21875, ((0, 64),))
    return dict(query=query, keys=keys, values=values, lengths=lengths, routes=routes, gates=gates, norm_gain=norm_gain, old_holds=old_holds, dup_experts=dup_experts, w_gate=w_gate, w_up=w_up, w_down=w_down)


def attend(query, key_rows, value_rows, lengths):
    rows = query.shape[0]
    kv_heads = key_rows.shape[1] // HEAD_WIDTH
    query_group = query.shape[1] // HEAD_WIDTH // kv_heads
    ends = jnp.cumsum(lengths)
    position = lax.iota(jnp.int32, rows)
    request = lax.optimization_barrier(jnp.sum((position[:, None] >= ends[None, :]).astype(jnp.int32), axis=1))
    allowed = (request[:, None] == request[None, :]) & (position[None, :] <= position[:, None])
    query_heads = query.reshape(rows, kv_heads, query_group, HEAD_WIDTH).astype(jnp.float32)
    key_heads = key_rows.reshape(rows, kv_heads, HEAD_WIDTH).astype(jnp.float32)
    value_heads = value_rows.reshape(rows, kv_heads, HEAD_WIDTH).astype(jnp.float32)
    router_logits = jnp.einsum('qhgd,khd->hgqk', query_heads, key_heads) * HEAD_WIDTH ** (-0.5)
    router_logits = jnp.where(allowed[None, None], router_logits, -1e+30)
    highest = lax.optimization_barrier(jnp.max(router_logits, axis=-1, keepdims=True))
    weights = jnp.exp(router_logits - highest)
    probs = (weights / lax.optimization_barrier(jnp.sum(weights, axis=-1, keepdims=True))).astype(jnp.bfloat16)
    mixed = jnp.einsum('hgqk,khd->qhgd', probs.astype(jnp.float32), value_heads)
    return mixed.reshape(rows, kv_heads * query_group * HEAD_WIDTH)

def normalize(attn, gain):
    meansq = lax.optimization_barrier(jnp.mean(attn * attn, axis=-1, keepdims=True))
    return (attn * lax.rsqrt(meansq + 1e-05) * gain).astype(jnp.bfloat16)

def expert_rows(rows, gate_mat, up_mat, down_mat):
    gate_val = jnp.dot(rows, gate_mat, preferred_element_type=jnp.float32)
    up_val = jnp.dot(rows, up_mat, preferred_element_type=jnp.float32)
    hidden = (jax.nn.silu(gate_val) * up_val).astype(jnp.bfloat16)
    return jnp.dot(hidden, down_mat, preferred_element_type=jnp.float32).astype(jnp.bfloat16)

def positions(routes, copies_of):
    expert_list = lax.iota(jnp.int32, copies_of.shape[0])
    hit = (routes[:, :, None] == expert_list[None, None, :]).astype(jnp.int32)
    named = lax.optimization_barrier(jnp.sum(hit, axis=1))
    before = jnp.cumsum(named, axis=0) - named
    place = lax.optimization_barrier(jnp.sum(hit * before[:, None, :], axis=2))
    limit = lax.optimization_barrier(jnp.sum(hit * copies_of[None, None, :], axis=2))
    return (place, place < limit * CAP)

def block_attention(parts):
    return attend(parts[0], parts[1], parts[2], parts[3])

def one_batch(query, keys, values, lengths, routes, gates, gain, holder, copies_of, w_gate, w_up, w_down):
    count = BATCH_TOKENS // TOK
    attn = lax.map(block_attention, (query.reshape(count, TOK, -1), keys.reshape(count, TOK, -1), values.reshape(count, TOK, -1), lengths))
    attn = attn.reshape(BATCH_TOKENS, -1)
    normed = normalize(attn, gain)
    block_routes = routes.reshape(count, TOK, TOPK)
    place, kept = jax.vmap(lambda selected_experts: positions(selected_experts, copies_of))(block_routes)
    source = lax.iota(jnp.int32, count)[:, None, None]
    row_index = lax.iota(jnp.int32, TOK)[None, :, None]
    width = count * 2 * CAP
    column = source * (2 * CAP) + place
    expert = jnp.where(kept, block_routes, EXPERTS)
    token = jnp.broadcast_to(source * TOK + row_index, place.shape).astype(jnp.int32)
    table_rows = jnp.full((EXPERTS, width), BATCH_TOKENS, jnp.int32).at[expert, column].set(token, mode='drop')
    table_gate = jnp.zeros((EXPERTS, width), jnp.float32).at[expert, column].set(gates.reshape(count, TOK, TOPK), mode='drop')
    padded = jnp.concatenate([normed, jnp.zeros((1, normed.shape[1]), normed.dtype)], axis=0)

    def step(total, index):
        slot = holder[index]
        picked = table_rows[index]
        rows = padded[picked]
        result = expert_rows(rows, w_gate[slot], w_up[slot], w_down[slot])
        total = total.at[picked].add(table_gate[index][:, None] * result.astype(jnp.float32))
        return (total, None)
    total, _ = lax.scan(step, jnp.zeros((BATCH_TOKENS + 1, normed.shape[1]), jnp.float32), lax.iota(jnp.int32, EXPERTS))
    return (attn + total[:BATCH_TOKENS]).astype(jnp.bfloat16)

def reference(query, keys, values, lengths, routes, gates, norm_gain, old_holds, dup_experts, w_gate, w_up, w_down):
    expert_list = lax.iota(jnp.int32, EXPERTS)
    holder = lax.optimization_barrier(jnp.sum(expert_list[:, None] * (old_holds[:, None] == expert_list[None, :]).astype(jnp.int32), axis=0))
    doubled = lax.optimization_barrier(jnp.sum((dup_experts[:, None] == expert_list[None, :]).astype(jnp.int32), axis=0))
    first = one_batch(query[0], keys[0], values[0], lengths[0], routes[0], gates[0], norm_gain, holder, jnp.ones_like(doubled), w_gate, w_up, w_down)
    second = one_batch(query[1], keys[1], values[1], lengths[1], routes[1], gates[1], norm_gain, holder, 1 + doubled, w_gate, w_up, w_down)
    return jnp.stack([first, second])
```

```python
import jax
import jax.numpy as jnp
from jax import lax
from jax.sharding import PartitionSpec as P

HEAD_WIDTH = 128
CAP = 6


def attend(query, key_rows, value_rows, lengths):
    rows = query.shape[0]
    kv_heads = key_rows.shape[1] // HEAD_WIDTH
    query_group = query.shape[1] // HEAD_WIDTH // kv_heads
    ends = jnp.cumsum(lengths)
    position = lax.iota(jnp.int32, rows)
    request = jnp.sum((position[:, None] >= ends[None, :]).astype(jnp.int32), axis=1)
    allowed = (request[:, None] == request[None, :]) & (position[None, :] <= position[:, None])
    query_heads = query.reshape(rows, kv_heads, query_group, HEAD_WIDTH)
    key_heads = key_rows.reshape(rows, kv_heads, HEAD_WIDTH)
    value_heads = value_rows.reshape(rows, kv_heads, HEAD_WIDTH)
    router_logits = jnp.einsum(
        "qhgd,khd->hgqk", query_heads, key_heads, preferred_element_type=jnp.float32
    ) * HEAD_WIDTH ** (-0.5)
    router_logits = jnp.where(allowed[None, None], router_logits, -1e30)
    highest = jnp.max(router_logits, axis=-1, keepdims=True)
    weights = jnp.exp(router_logits - highest)
    probs = (weights / jnp.sum(weights, axis=-1, keepdims=True)).astype(jnp.bfloat16)
    mixed = jnp.einsum("hgqk,khd->qhgd", probs, value_heads, preferred_element_type=jnp.float32)
    return mixed.reshape(rows, kv_heads * query_group * HEAD_WIDTH)


def normalize(attn, gain):
    meansq = jnp.mean(attn * attn, axis=-1, keepdims=True)
    return (attn * lax.rsqrt(meansq + 1e-05) * gain).astype(jnp.bfloat16)


def expert_rows(rows, gate_mat, up_mat, down_mat):
    gate_val = jnp.dot(rows, gate_mat, preferred_element_type=jnp.float32)
    up_val = jnp.dot(rows, up_mat, preferred_element_type=jnp.float32)
    hidden = (jax.nn.silu(gate_val) * up_val).astype(jnp.bfloat16)
    return jnp.dot(hidden, down_mat, preferred_element_type=jnp.float32).astype(jnp.bfloat16)


def routing(routes, copies_of, holder):
    expert_list = lax.iota(jnp.int32, copies_of.shape[0])
    hit = (routes[:, :, None] == expert_list[None, None, :]).astype(jnp.int32)
    named = jnp.sum(hit, axis=1)
    before = jnp.cumsum(named, axis=0) - named
    place = jnp.sum(hit * before[:, None, :], axis=2)
    limit = jnp.sum(hit * copies_of[None, None, :], axis=2)
    kept = place < limit * CAP
    target = jnp.sum(hit * holder[None, None, :], axis=2)
    return (target, place, kept)


def combine(attn, returned, spot, kept, gates):
    picked = returned[jnp.minimum(spot, returned.shape[0] - 1)]
    weight = jnp.where(kept, gates, 0.0)
    mixed = jnp.einsum("tk,tkd->td", weight, picked.astype(jnp.float32))
    return (attn + mixed).astype(jnp.bfloat16)


def shards(
    query,
    keys,
    values,
    lengths,
    routes,
    gates,
    norm_gain,
    old_holds,
    dup_experts,
    w_gate,
    w_up,
    w_down,
):
    width = lax.axis_size("expert")
    features = norm_gain.shape[0]
    tokens = query.shape[1]
    per_dest = 3 * CAP
    slots = width * per_dest
    expert_list = lax.iota(jnp.int32, old_holds.shape[0])
    holder = jnp.sum(
        expert_list[:, None] * (old_holds[:, None] == expert_list[None, :]).astype(jnp.int32),
        axis=0,
    )
    doubled = jnp.sum((dup_experts[:, None] == expert_list[None, :]).astype(jnp.int32), axis=0)
    attn_one = attend(query[0], keys[0], values[0], lengths[0, 0])
    attn_two = attend(query[1], keys[1], values[1], lengths[1, 0])
    normed = normalize(jnp.concatenate([attn_one, attn_two], axis=0), norm_gain)
    target_one, place_one, kept_one = routing(routes[0], jnp.ones_like(doubled), holder)
    target_two, place_two, kept_two = routing(routes[1], 1 + doubled, holder)
    spot_one = jnp.where(kept_one, target_one * per_dest + place_one, slots)
    spot_two = jnp.where(kept_two, target_two * per_dest + CAP + place_two, slots)
    token = lax.iota(jnp.int32, tokens)[:, None]
    token_one = jnp.broadcast_to(token, spot_one.shape)
    token_two = jnp.broadcast_to(token + tokens, spot_two.shape)
    source_row = (
        jnp.full((slots,), 2 * tokens, jnp.int32)
        .at[spot_one].set(token_one, mode="drop")
        .at[spot_two].set(token_two, mode="drop")
    )
    padded = jnp.concatenate([normed, jnp.zeros((1, features), normed.dtype)], axis=0)
    packed = padded[source_row]
    received = lax.all_to_all(
        packed.reshape(width, per_dest, features),
        "expert",
        split_axis=0,
        concat_axis=0,
        tiled=True,
    )
    result = expert_rows(received.reshape(-1, features), w_gate[0], w_up[0], w_down[0])
    back = lax.all_to_all(
        result.reshape(received.shape), "expert", split_axis=0, concat_axis=0, tiled=True
    ).reshape(-1, features)
    out_one = combine(attn_one, back, spot_one, kept_one, gates[0])
    out_two = combine(attn_two, back, spot_two, kept_two, gates[1])
    return jnp.stack([out_one, out_two])


def solution(mesh):
    placed = (
        P(None, ("dp", "expert"), None),
        P(None, ("dp", "expert"), None),
        P(None, ("dp", "expert"), None),
        P(None, ("dp", "expert"), None),
        P(None, ("dp", "expert"), None),
        P(None, ("dp", "expert"), None),
        P(),
        P(),
        P(),
        P("expert", None, None),
        P("expert", None, None),
        P("expert", None, None),
    )
    return jax.shard_map(
        shards,
        mesh=mesh,
        in_specs=placed,
        out_specs=P(None, ("dp", "expert"), None),
        check_vma=False,
    )
```

```python
import jax
import jax.numpy as jnp
from jax import lax
from jax.sharding import PartitionSpec as P

HEAD_WIDTH = 128
CAP = 6


def attend(query, key_rows, value_rows, lengths):
    rows = query.shape[0]
    kv_heads = key_rows.shape[1] // HEAD_WIDTH
    query_group = query.shape[1] // HEAD_WIDTH // kv_heads
    ends = jnp.cumsum(lengths)
    position = lax.iota(jnp.int32, rows)
    request = jnp.sum((position[:, None] >= ends[None, :]).astype(jnp.int32), axis=1)
    allowed = (request[:, None] == request[None, :]) & (position[None, :] <= position[:, None])
    query_heads = query.reshape(rows, kv_heads, query_group, HEAD_WIDTH)
    key_heads = key_rows.reshape(rows, kv_heads, HEAD_WIDTH)
    value_heads = value_rows.reshape(rows, kv_heads, HEAD_WIDTH)
    router_logits = jnp.einsum(
        "qhgd,khd->hgqk", query_heads, key_heads, preferred_element_type=jnp.float32
    ) * HEAD_WIDTH ** (-0.5)
    router_logits = jnp.where(allowed[None, None], router_logits, -1e30)
    highest = jnp.max(router_logits, axis=-1, keepdims=True)
    weights = jnp.exp(router_logits - highest)
    probs = (weights / jnp.sum(weights, axis=-1, keepdims=True)).astype(jnp.bfloat16)
    mixed = jnp.einsum("hgqk,khd->qhgd", probs, value_heads, preferred_element_type=jnp.float32)
    return mixed.reshape(rows, kv_heads * query_group * HEAD_WIDTH)


def normalize(attn, gain):
    meansq = jnp.mean(attn * attn, axis=-1, keepdims=True)
    return (attn * lax.rsqrt(meansq + 1e-05) * gain).astype(jnp.bfloat16)


def expert_rows(rows, gate_mat, up_mat, down_mat):
    gate_val = jnp.dot(rows, gate_mat, preferred_element_type=jnp.float32)
    up_val = jnp.dot(rows, up_mat, preferred_element_type=jnp.float32)
    hidden = (jax.nn.silu(gate_val) * up_val).astype(jnp.bfloat16)
    return jnp.dot(hidden, down_mat, preferred_element_type=jnp.float32).astype(jnp.bfloat16)


def routing(routes, copies_of, first_target, second_target, regions):
    expert_list = lax.iota(jnp.int32, copies_of.shape[0])
    hit = (routes[:, :, None] == expert_list[None, None, :]).astype(jnp.int32)
    named = jnp.sum(hit, axis=1)
    before = jnp.cumsum(named, axis=0) - named
    place = jnp.sum(hit * before[:, None, :], axis=2)
    limit = jnp.sum(hit * copies_of[None, None, :], axis=2)
    kept = place < limit * CAP
    which = place // CAP
    target = jnp.where(
        which == 0,
        jnp.sum(hit * first_target[None, None, :], axis=2),
        jnp.sum(hit * second_target[None, None, :], axis=2),
    )
    flat = (target * regions + which) * CAP + place % CAP
    return (flat, kept)


def pack(normed, flat, kept, slots):
    tok_rows = normed.shape[0]
    token = jnp.broadcast_to(lax.iota(jnp.int32, tok_rows)[:, None], flat.shape)
    spot = jnp.where(kept, flat, slots)
    source_row = jnp.full((slots,), tok_rows, jnp.int32).at[spot].set(token, mode="drop")
    padded = jnp.concatenate([normed, jnp.zeros((1, normed.shape[1]), normed.dtype)], axis=0)
    return (padded[source_row], spot)


def combine(attn, returned, spot, kept, gates):
    picked = returned[jnp.minimum(spot, returned.shape[0] - 1)]
    weight = jnp.where(kept, gates, 0.0)
    mixed = jnp.einsum("tk,tkd->td", weight, picked.astype(jnp.float32))
    return (attn + mixed).astype(jnp.bfloat16)


def shards(
    query,
    keys,
    values,
    lengths,
    routes,
    gates,
    norm_gain,
    old_holds,
    dup_experts,
    w_gate,
    w_up,
    w_down,
):
    width = lax.axis_size("expert")
    features = norm_gain.shape[0]
    expert_list = lax.iota(jnp.int32, old_holds.shape[0])
    holder = jnp.sum(
        expert_list[:, None] * (old_holds[:, None] == expert_list[None, :]).astype(jnp.int32),
        axis=0,
    )
    doubled = jnp.sum((dup_experts[:, None] == expert_list[None, :]).astype(jnp.int32), axis=0)
    own_gate, own_up, own_down = (w_gate[0], w_up[0], w_down[0])
    attn_one = attend(query[0], keys[0], values[0], lengths[0, 0])
    normed_one = normalize(attn_one, norm_gain)
    flat_one, kept_one = routing(routes[0], jnp.ones_like(doubled), holder, holder, 1)
    packed_one, spot_one = pack(normed_one, flat_one, kept_one, width * CAP)
    received = lax.all_to_all(
        packed_one.reshape(width, 1, CAP, features),
        "expert",
        split_axis=0,
        concat_axis=0,
        tiled=True,
    )
    result = expert_rows(received.reshape(-1, features), own_gate, own_up, own_down)
    back_one = lax.all_to_all(
        result.reshape(received.shape), "expert", split_axis=0, concat_axis=0, tiled=True
    )
    out_one = combine(attn_one, back_one.reshape(-1, features), spot_one, kept_one, gates[0])
    attn_two = attend(query[1], keys[1], values[1], lengths[1, 0])
    normed_two = normalize(attn_two, norm_gain)
    flat_two, kept_two = routing(routes[1], 1 + doubled, holder, holder, 2)
    packed_two, spot_two = pack(normed_two, flat_two, kept_two, width * 2 * CAP)
    received = lax.all_to_all(
        packed_two.reshape(width, 2, CAP, features),
        "expert",
        split_axis=0,
        concat_axis=0,
        tiled=True,
    )
    result = expert_rows(received.reshape(-1, features), own_gate, own_up, own_down).reshape(
        received.shape
    )
    back_two = lax.all_to_all(result, "expert", split_axis=0, concat_axis=0, tiled=True)
    out_two = combine(attn_two, back_two.reshape(-1, features), spot_two, kept_two, gates[1])
    return jnp.stack([out_one, out_two])


def solution(mesh):
    placed = (
        P(None, ("dp", "expert"), None),
        P(None, ("dp", "expert"), None),
        P(None, ("dp", "expert"), None),
        P(None, ("dp", "expert"), None),
        P(None, ("dp", "expert"), None),
        P(None, ("dp", "expert"), None),
        P(),
        P(),
        P(),
        P("expert", None, None),
        P("expert", None, None),
        P("expert", None, None),
    )
    return jax.shard_map(
        shards,
        mesh=mesh,
        in_specs=placed,
        out_specs=P(None, ("dp", "expert"), None),
        check_vma=False,
    )
```

```python
import jax
import jax.numpy as jnp
from jax import lax
from jax.sharding import PartitionSpec as P
from jax.experimental import pallas as pl
from jax.experimental.pallas import tpu as pltpu

HEAD_WIDTH = 128
CAP = 6


def exchange_kernel(x_ref, o_ref, send_sem, recv_sem, local_sem):
    me = lax.axis_index("expert")
    width = x_ref.shape[0]

    def remote(target, slot):
        return pltpu.make_async_remote_copy(
            src_ref=x_ref.at[target],
            dst_ref=o_ref.at[slot],
            send_sem=send_sem.at[target],
            recv_sem=recv_sem.at[slot],
            device_id={"expert": target},
            device_id_type=pl.DeviceIdType.MESH,
        )

    local = pltpu.make_async_copy(x_ref.at[me], o_ref.at[me], local_sem)
    local.start()

    def start(step, carry):
        remote(lax.rem(me + step, width), me).start()
        return carry

    lax.fori_loop(1, width, start, 0)

    def finish(step, carry):
        remote(lax.rem(me + step, width), me).wait_send()
        remote(me, lax.rem(me + width - step, width)).wait_recv()
        return carry

    lax.fori_loop(1, width, finish, 0)
    local.wait()


def exchange(x):
    width = x.shape[0]
    return pl.pallas_call(
        exchange_kernel,
        out_shape=jax.ShapeDtypeStruct(x.shape, x.dtype),
        in_specs=[pl.BlockSpec(memory_space=pl.ANY)],
        out_specs=pl.BlockSpec(memory_space=pl.ANY),
        scratch_shapes=[
            pltpu.SemaphoreType.DMA((width,)),
            pltpu.SemaphoreType.DMA((width,)),
            pltpu.SemaphoreType.DMA,
        ],
        compiler_params=pltpu.CompilerParams(has_side_effects=True),
    )(x)


def attend(query, key_rows, value_rows, lengths):
    rows = query.shape[0]
    kv_heads = key_rows.shape[1] // HEAD_WIDTH
    query_group = query.shape[1] // HEAD_WIDTH // kv_heads
    ends = jnp.cumsum(lengths)
    position = lax.iota(jnp.int32, rows)
    request = jnp.sum((position[:, None] >= ends[None, :]).astype(jnp.int32), axis=1)
    allowed = (request[:, None] == request[None, :]) & (position[None, :] <= position[:, None])
    query_heads = query.reshape(rows, kv_heads, query_group, HEAD_WIDTH)
    key_heads = key_rows.reshape(rows, kv_heads, HEAD_WIDTH)
    value_heads = value_rows.reshape(rows, kv_heads, HEAD_WIDTH)
    router_logits = jnp.einsum(
        "qhgd,khd->hgqk", query_heads, key_heads, preferred_element_type=jnp.float32
    ) * HEAD_WIDTH ** (-0.5)
    router_logits = jnp.where(allowed[None, None], router_logits, -1e30)
    highest = jnp.max(router_logits, axis=-1, keepdims=True)
    weights = jnp.exp(router_logits - highest)
    probs = (weights / jnp.sum(weights, axis=-1, keepdims=True)).astype(jnp.bfloat16)
    mixed = jnp.einsum("hgqk,khd->qhgd", probs, value_heads, preferred_element_type=jnp.float32)
    return mixed.reshape(rows, kv_heads * query_group * HEAD_WIDTH)


def normalize(attn, gain):
    meansq = jnp.mean(attn * attn, axis=-1, keepdims=True)
    return (attn * lax.rsqrt(meansq + 1e-05) * gain).astype(jnp.bfloat16)


def expert_rows(rows, gate_mat, up_mat, down_mat):
    gate_val = jnp.dot(rows, gate_mat, preferred_element_type=jnp.float32)
    up_val = jnp.dot(rows, up_mat, preferred_element_type=jnp.float32)
    hidden = (jax.nn.silu(gate_val) * up_val).astype(jnp.bfloat16)
    return jnp.dot(hidden, down_mat, preferred_element_type=jnp.float32).astype(jnp.bfloat16)


def routing(routes, copies_of, first_target, second_target, regions):
    expert_list = lax.iota(jnp.int32, copies_of.shape[0])
    hit = (routes[:, :, None] == expert_list[None, None, :]).astype(jnp.int32)
    named = jnp.sum(hit, axis=1)
    before = jnp.cumsum(named, axis=0) - named
    place = jnp.sum(hit * before[:, None, :], axis=2)
    limit = jnp.sum(hit * copies_of[None, None, :], axis=2)
    kept = place < limit * CAP
    which = place // CAP
    target = jnp.where(
        which == 0,
        jnp.sum(hit * first_target[None, None, :], axis=2),
        jnp.sum(hit * second_target[None, None, :], axis=2),
    )
    flat = (target * regions + which) * CAP + place % CAP
    return (flat, kept)


def pack(normed, flat, kept, slots):
    tok_rows = normed.shape[0]
    token = jnp.broadcast_to(lax.iota(jnp.int32, tok_rows)[:, None], flat.shape)
    spot = jnp.where(kept, flat, slots)
    source_row = jnp.full((slots,), tok_rows, jnp.int32).at[spot].set(token, mode="drop")
    padded = jnp.concatenate([normed, jnp.zeros((1, normed.shape[1]), normed.dtype)], axis=0)
    return (padded[source_row], spot)


def combine(attn, returned, spot, kept, gates):
    picked = returned[jnp.minimum(spot, returned.shape[0] - 1)]
    weight = jnp.where(kept, gates, 0.0)
    mixed = jnp.einsum("tk,tkd->td", weight, picked.astype(jnp.float32))
    return (attn + mixed).astype(jnp.bfloat16)


def shards(
    query,
    keys,
    values,
    lengths,
    routes,
    gates,
    norm_gain,
    old_holds,
    dup_experts,
    w_gate,
    w_up,
    w_down,
):
    width = lax.axis_size("expert")
    features = norm_gain.shape[0]
    expert_list = lax.iota(jnp.int32, old_holds.shape[0])
    holder = jnp.sum(
        expert_list[:, None] * (old_holds[:, None] == expert_list[None, :]).astype(jnp.int32),
        axis=0,
    )
    doubled = jnp.sum((dup_experts[:, None] == expert_list[None, :]).astype(jnp.int32), axis=0)
    own_gate, own_up, own_down = (w_gate[0], w_up[0], w_down[0])
    attn_one = attend(query[0], keys[0], values[0], lengths[0, 0])
    normed_one = normalize(attn_one, norm_gain)
    flat_one, kept_one = routing(routes[0], jnp.ones_like(doubled), holder, holder, 1)
    packed_one, spot_one = pack(normed_one, flat_one, kept_one, width * CAP)
    received = exchange(packed_one.reshape(width, CAP, features))
    result = expert_rows(received.reshape(-1, features), own_gate, own_up, own_down)
    back_one = exchange(result.reshape(received.shape))
    out_one = combine(attn_one, back_one.reshape(-1, features), spot_one, kept_one, gates[0])
    attn_two = attend(query[1], keys[1], values[1], lengths[1, 0])
    normed_two = normalize(attn_two, norm_gain)
    flat_two, kept_two = routing(routes[1], 1 + doubled, holder, holder, 2)
    packed_two, spot_two = pack(normed_two, flat_two, kept_two, width * 2 * CAP)
    received = exchange(packed_two.reshape(width, 2 * CAP, features))
    result = expert_rows(received.reshape(-1, features), own_gate, own_up, own_down).reshape(
        received.shape
    )
    back_two = exchange(result)
    out_two = combine(attn_two, back_two.reshape(-1, features), spot_two, kept_two, gates[1])
    return jnp.stack([out_one, out_two])


def solution(mesh):
    placed = (
        P(None, ("dp", "expert"), None),
        P(None, ("dp", "expert"), None),
        P(None, ("dp", "expert"), None),
        P(None, ("dp", "expert"), None),
        P(None, ("dp", "expert"), None),
        P(None, ("dp", "expert"), None),
        P(),
        P(),
        P(),
        P("expert", None, None),
        P("expert", None, None),
        P("expert", None, None),
    )
    return jax.shard_map(
        shards,
        mesh=mesh,
        in_specs=placed,
        out_specs=P(None, ("dp", "expert"), None),
        check_vma=False,
    )
```

```python
import jax
import jax.numpy as jnp
from jax import lax
from jax.sharding import PartitionSpec as P

HEAD_WIDTH = 128
CAP = 6
ROW_TILE = 8


def attend(query, key_rows, value_rows, lengths):
    rows = query.shape[0]
    kv_heads = key_rows.shape[1] // HEAD_WIDTH
    query_group = query.shape[1] // HEAD_WIDTH // kv_heads
    ends = jnp.cumsum(lengths)
    position = lax.iota(jnp.int32, rows)
    request = jnp.sum((position[:, None] >= ends[None, :]).astype(jnp.int32), axis=1)
    allowed = (request[:, None] == request[None, :]) & (position[None, :] <= position[:, None])
    query_heads = query.reshape(rows, kv_heads, query_group, HEAD_WIDTH)
    key_heads = key_rows.reshape(rows, kv_heads, HEAD_WIDTH)
    value_heads = value_rows.reshape(rows, kv_heads, HEAD_WIDTH)
    router_logits = jnp.einsum(
        "qhgd,khd->hgqk", query_heads, key_heads, preferred_element_type=jnp.float32
    ) * HEAD_WIDTH ** (-0.5)
    router_logits = jnp.where(allowed[None, None], router_logits, -1e30)
    highest = jnp.max(router_logits, axis=-1, keepdims=True)
    weights = jnp.exp(router_logits - highest)
    probs = (weights / jnp.sum(weights, axis=-1, keepdims=True)).astype(jnp.bfloat16)
    mixed = jnp.einsum("hgqk,khd->qhgd", probs, value_heads, preferred_element_type=jnp.float32)
    return mixed.reshape(rows, kv_heads * query_group * HEAD_WIDTH)


def normalize(attn, gain):
    meansq = jnp.mean(attn * attn, axis=-1, keepdims=True)
    return (attn * lax.rsqrt(meansq + 1e-05) * gain).astype(jnp.bfloat16)


def expert_rows(rows, gate_mat, up_mat, down_mat):
    gate_val = jnp.dot(rows, gate_mat, preferred_element_type=jnp.float32)
    up_val = jnp.dot(rows, up_mat, preferred_element_type=jnp.float32)
    hidden = (jax.nn.silu(gate_val) * up_val).astype(jnp.bfloat16)
    return jnp.dot(hidden, down_mat, preferred_element_type=jnp.float32).astype(jnp.bfloat16)


def routing(routes, copies_of, first_target, stride):
    expert_list = lax.iota(jnp.int32, copies_of.shape[0])
    hit = (routes[:, :, None] == expert_list[None, None, :]).astype(jnp.int32)
    named = jnp.sum(hit, axis=1)
    before = jnp.cumsum(named, axis=0) - named
    place = jnp.sum(hit * before[:, None, :], axis=2)
    limit = jnp.sum(hit * copies_of[None, None, :], axis=2)
    kept = place < limit * CAP
    target = jnp.sum(hit * first_target[None, None, :], axis=2)
    flat = target * stride + place
    return (flat, kept)


def pack(normed, flat, kept, slots):
    tok_rows = normed.shape[0]
    token = jnp.broadcast_to(lax.iota(jnp.int32, tok_rows)[:, None], flat.shape)
    spot = jnp.where(kept, flat, slots)
    source_row = jnp.full((slots,), tok_rows, jnp.int32).at[spot].set(token, mode="drop")
    padded = jnp.concatenate([normed, jnp.zeros((1, normed.shape[1]), normed.dtype)], axis=0)
    return (padded[source_row], spot)


def combine(attn, returned, spot, kept, gates):
    picked = returned[jnp.minimum(spot, returned.shape[0] - 1)]
    weight = jnp.where(kept, gates, 0.0)
    mixed = jnp.einsum("tk,tkd->td", weight, picked.astype(jnp.float32))
    return (attn + mixed).astype(jnp.bfloat16)


def shards(
    query,
    keys,
    values,
    lengths,
    routes,
    gates,
    norm_gain,
    old_holds,
    dup_experts,
    w_gate,
    w_up,
    w_down,
):
    width = lax.axis_size("expert")
    features = norm_gain.shape[0]
    expert_list = lax.iota(jnp.int32, old_holds.shape[0])
    holder = jnp.sum(
        expert_list[:, None] * (old_holds[:, None] == expert_list[None, :]).astype(jnp.int32),
        axis=0,
    )
    doubled = jnp.sum((dup_experts[:, None] == expert_list[None, :]).astype(jnp.int32), axis=0)
    own_gate, own_up, own_down = (w_gate[0], w_up[0], w_down[0])
    attn_one = attend(query[0], keys[0], values[0], lengths[0, 0])
    normed_one = normalize(attn_one, norm_gain)
    flat_one, kept_one = routing(routes[0], jnp.ones_like(doubled), holder, ROW_TILE)
    packed_one, spot_one = pack(normed_one, flat_one, kept_one, width * ROW_TILE)
    received = lax.all_to_all(
        packed_one.reshape(width, ROW_TILE, features),
        "expert",
        split_axis=0,
        concat_axis=0,
        tiled=True,
    )
    result = expert_rows(received.reshape(-1, features), own_gate, own_up, own_down)
    back_one = lax.all_to_all(
        result.reshape(received.shape), "expert", split_axis=0, concat_axis=0, tiled=True
    )
    out_one = combine(attn_one, back_one.reshape(-1, features), spot_one, kept_one, gates[0])
    attn_two = attend(query[1], keys[1], values[1], lengths[1, 0])
    normed_two = normalize(attn_two, norm_gain)
    flat_two, kept_two = routing(routes[1], 1 + doubled, holder, 2 * ROW_TILE)
    packed_two, spot_two = pack(normed_two, flat_two, kept_two, width * 2 * ROW_TILE)
    received = lax.all_to_all(
        packed_two.reshape(width, 2 * ROW_TILE, features),
        "expert",
        split_axis=0,
        concat_axis=0,
        tiled=True,
    )
    result = expert_rows(received.reshape(-1, features), own_gate, own_up, own_down).reshape(
        received.shape
    )
    back_two = lax.all_to_all(result, "expert", split_axis=0, concat_axis=0, tiled=True)
    out_two = combine(attn_two, back_two.reshape(-1, features), spot_two, kept_two, gates[1])
    return jnp.stack([out_one, out_two])


def solution(mesh):
    placed = (
        P(None, ("dp", "expert"), None),
        P(None, ("dp", "expert"), None),
        P(None, ("dp", "expert"), None),
        P(None, ("dp", "expert"), None),
        P(None, ("dp", "expert"), None),
        P(None, ("dp", "expert"), None),
        P(),
        P(),
        P(),
        P("expert", None, None),
        P("expert", None, None),
        P("expert", None, None),
    )
    return jax.shard_map(
        shards,
        mesh=mesh,
        in_specs=placed,
        out_specs=P(None, ("dp", "expert"), None),
        check_vma=False,
    )
```

```python
import jax
import jax.numpy as jnp
from jax import lax
from jax.sharding import PartitionSpec as P

HEAD_WIDTH = 128
CAP = 6


def attend(query, key_rows, value_rows, lengths):
    rows = query.shape[0]
    kv_heads = key_rows.shape[1] // HEAD_WIDTH
    query_group = query.shape[1] // HEAD_WIDTH // kv_heads
    ends = jnp.cumsum(lengths)
    position = lax.iota(jnp.int32, rows)
    request = jnp.sum((position[:, None] >= ends[None, :]).astype(jnp.int32), axis=1)
    allowed = (request[:, None] == request[None, :]) & (position[None, :] <= position[:, None])
    query_heads = query.reshape(rows, kv_heads, query_group, HEAD_WIDTH)
    key_heads = key_rows.reshape(rows, kv_heads, HEAD_WIDTH)
    value_heads = value_rows.reshape(rows, kv_heads, HEAD_WIDTH)
    router_logits = jnp.einsum(
        "qhgd,khd->hgqk", query_heads, key_heads, preferred_element_type=jnp.float32
    ) * HEAD_WIDTH ** (-0.5)
    router_logits = jnp.where(allowed[None, None], router_logits, -1e30)
    highest = jnp.max(router_logits, axis=-1, keepdims=True)
    weights = jnp.exp(router_logits - highest)
    probs = (weights / jnp.sum(weights, axis=-1, keepdims=True)).astype(jnp.bfloat16)
    mixed = jnp.einsum("hgqk,khd->qhgd", probs, value_heads, preferred_element_type=jnp.float32)
    return mixed.reshape(rows, kv_heads * query_group * HEAD_WIDTH)


def normalize(attn, gain):
    meansq = jnp.mean(attn * attn, axis=-1, keepdims=True)
    return (attn * lax.rsqrt(meansq + 1e-05) * gain).astype(jnp.bfloat16)


def expert_rows(rows, gate_mat, up_mat, down_mat):
    gate_val = jnp.dot(rows, gate_mat, preferred_element_type=jnp.float32)
    up_val = jnp.dot(rows, up_mat, preferred_element_type=jnp.float32)
    hidden = (jax.nn.silu(gate_val) * up_val).astype(jnp.bfloat16)
    return jnp.dot(hidden, down_mat, preferred_element_type=jnp.float32).astype(jnp.bfloat16)


def routing(routes, copies_of, first_target, second_target, regions):
    expert_list = lax.iota(jnp.int32, copies_of.shape[0])
    hit = (routes[:, :, None] == expert_list[None, None, :]).astype(jnp.int32)
    named = jnp.sum(hit, axis=1)
    before = jnp.cumsum(named, axis=0) - named
    place = jnp.sum(hit * before[:, None, :], axis=2)
    limit = jnp.sum(hit * copies_of[None, None, :], axis=2)
    kept = place < limit * CAP
    which = place // CAP
    target = jnp.where(
        which == 0,
        jnp.sum(hit * first_target[None, None, :], axis=2),
        jnp.sum(hit * second_target[None, None, :], axis=2),
    )
    flat = (target * regions + which) * CAP + place % CAP
    return (flat, kept)


def pack(normed, flat, kept, slots):
    tok_rows = normed.shape[0]
    token = jnp.broadcast_to(lax.iota(jnp.int32, tok_rows)[:, None], flat.shape)
    spot = jnp.where(kept, flat, slots)
    source_row = jnp.full((slots,), tok_rows, jnp.int32).at[spot].set(token, mode="drop")
    padded = jnp.concatenate([normed, jnp.zeros((1, normed.shape[1]), normed.dtype)], axis=0)
    return (padded[source_row], spot)


def combine(attn, returned, spot, kept, gates):
    picked = returned[jnp.minimum(spot, returned.shape[0] - 1)]
    weight = jnp.where(kept, gates, 0.0)
    mixed = jnp.einsum("tk,tkd->td", weight, picked.astype(jnp.float32))
    return (attn + mixed).astype(jnp.bfloat16)


def shards(
    query,
    keys,
    values,
    lengths,
    routes,
    gates,
    norm_gain,
    old_holds,
    dup_experts,
    w_gate,
    w_up,
    w_down,
):
    width = lax.axis_size("expert")
    features = norm_gain.shape[0]
    expert_list = lax.iota(jnp.int32, old_holds.shape[0])
    holder = jnp.sum(
        expert_list[:, None] * (old_holds[:, None] == expert_list[None, :]).astype(jnp.int32),
        axis=0,
    )
    doubled = jnp.sum((dup_experts[:, None] == expert_list[None, :]).astype(jnp.int32), axis=0)
    own_gate, own_up, own_down = (w_gate[0], w_up[0], w_down[0])
    attn_one = attend(query[0], keys[0], values[0], lengths[0, 0])
    attn_two = attend(query[1], keys[1], values[1], lengths[1, 0])
    normed_one = normalize(attn_one, norm_gain)
    normed_two = normalize(attn_two, norm_gain)
    flat_one, kept_one = routing(routes[0], jnp.ones_like(doubled), holder, holder, 1)
    flat_two, kept_two = routing(routes[1], 1 + doubled, holder, holder, 2)
    packed_one, spot_one = pack(normed_one, flat_one, kept_one, width * CAP)
    packed_two, spot_two = pack(normed_two, flat_two, kept_two, width * 2 * CAP)
    received_two = lax.all_to_all(
        packed_two.reshape(width, 2, CAP, features),
        "expert",
        split_axis=0,
        concat_axis=0,
        tiled=True,
    )
    packed_one, received_two = lax.optimization_barrier((packed_one, received_two))
    received_one = lax.all_to_all(
        packed_one.reshape(width, 1, CAP, features),
        "expert",
        split_axis=0,
        concat_axis=0,
        tiled=True,
    )
    result_two = expert_rows(
        received_two.reshape(-1, features), own_gate, own_up, own_down
    ).reshape(received_two.shape)
    result_two, received_one = lax.optimization_barrier((result_two, received_one))
    back_two = lax.all_to_all(result_two, "expert", split_axis=0, concat_axis=0, tiled=True)
    result_one = expert_rows(
        received_one.reshape(-1, features), own_gate, own_up, own_down
    ).reshape(received_one.shape)
    result_one, back_two = lax.optimization_barrier((result_one, back_two))
    back_one = lax.all_to_all(result_one, "expert", split_axis=0, concat_axis=0, tiled=True)
    out_two = combine(attn_two, back_two.reshape(-1, features), spot_two, kept_two, gates[1])
    out_one = combine(attn_one, back_one.reshape(-1, features), spot_one, kept_one, gates[0])
    return jnp.stack([out_one, out_two])


def solution(mesh):
    placed = (
        P(None, ("dp", "expert"), None),
        P(None, ("dp", "expert"), None),
        P(None, ("dp", "expert"), None),
        P(None, ("dp", "expert"), None),
        P(None, ("dp", "expert"), None),
        P(None, ("dp", "expert"), None),
        P(),
        P(),
        P(),
        P("expert", None, None),
        P("expert", None, None),
        P("expert", None, None),
    )
    return jax.shard_map(
        shards,
        mesh=mesh,
        in_specs=placed,
        out_specs=P(None, ("dp", "expert"), None),
        check_vma=False,
    )
```

```python
import jax
import jax.numpy as jnp
from jax import lax
from jax.sharding import PartitionSpec as P

HEAD_WIDTH = 128
CAP = 6


def attend(query, key_rows, value_rows, lengths):
    rows = query.shape[0]
    kv_heads = key_rows.shape[1] // HEAD_WIDTH
    query_group = query.shape[1] // HEAD_WIDTH // kv_heads
    ends = jnp.cumsum(lengths)
    position = lax.iota(jnp.int32, rows)
    request = jnp.sum((position[:, None] >= ends[None, :]).astype(jnp.int32), axis=1)
    allowed = (request[:, None] == request[None, :]) & (position[None, :] <= position[:, None])
    query_heads = query.reshape(rows, kv_heads, query_group, HEAD_WIDTH)
    key_heads = key_rows.reshape(rows, kv_heads, HEAD_WIDTH)
    value_heads = value_rows.reshape(rows, kv_heads, HEAD_WIDTH)
    router_logits = jnp.einsum(
        "qhgd,khd->hgqk", query_heads, key_heads, preferred_element_type=jnp.float32
    ) * HEAD_WIDTH ** (-0.5)
    router_logits = jnp.where(allowed[None, None], router_logits, -1e30)
    highest = jnp.max(router_logits, axis=-1, keepdims=True)
    weights = jnp.exp(router_logits - highest)
    probs = (weights / jnp.sum(weights, axis=-1, keepdims=True)).astype(jnp.bfloat16)
    mixed = jnp.einsum("hgqk,khd->qhgd", probs, value_heads, preferred_element_type=jnp.float32)
    return mixed.reshape(rows, kv_heads * query_group * HEAD_WIDTH)


def normalize(attn, gain):
    meansq = jnp.mean(attn * attn, axis=-1, keepdims=True)
    return (attn * lax.rsqrt(meansq + 1e-05) * gain).astype(jnp.bfloat16)


def expert_rows(rows, gate_mat, up_mat, down_mat):
    gate_val = jnp.dot(rows, gate_mat, preferred_element_type=jnp.float32)
    up_val = jnp.dot(rows, up_mat, preferred_element_type=jnp.float32)
    hidden = (jax.nn.silu(gate_val) * up_val).astype(jnp.bfloat16)
    return jnp.dot(hidden, down_mat, preferred_element_type=jnp.float32).astype(jnp.bfloat16)


def routing(routes, copies_of, first_target, second_target, regions):
    expert_list = lax.iota(jnp.int32, copies_of.shape[0])
    hit = (routes[:, :, None] == expert_list[None, None, :]).astype(jnp.int32)
    named = jnp.sum(hit, axis=1)
    before = jnp.cumsum(named, axis=0) - named
    place = jnp.sum(hit * before[:, None, :], axis=2)
    limit = jnp.sum(hit * copies_of[None, None, :], axis=2)
    kept = place < limit * CAP
    which = place // CAP
    target = jnp.where(
        which == 0,
        jnp.sum(hit * first_target[None, None, :], axis=2),
        jnp.sum(hit * second_target[None, None, :], axis=2),
    )
    flat = (target * regions + which) * CAP + place % CAP
    return (flat, kept)


def pack(normed, flat, kept, slots):
    tok_rows = normed.shape[0]
    token = jnp.broadcast_to(lax.iota(jnp.int32, tok_rows)[:, None], flat.shape)
    spot = jnp.where(kept, flat, slots)
    source_row = jnp.full((slots,), tok_rows, jnp.int32).at[spot].set(token, mode="drop")
    padded = jnp.concatenate([normed, jnp.zeros((1, normed.shape[1]), normed.dtype)], axis=0)
    return (padded[source_row], spot)


def combine(attn, returned, spot, kept, gates):
    where = jnp.minimum(spot, returned.size // returned.shape[-1] - 1)
    per_dest = returned.shape[1] * returned.shape[2]
    picked = returned[
        where // per_dest, (where % per_dest) // returned.shape[2], where % returned.shape[2]
    ]
    weight = jnp.where(kept, gates, 0.0)
    mixed = jnp.einsum("tk,tkd->td", weight, picked.astype(jnp.float32))
    return (attn + mixed).astype(jnp.bfloat16)


def shards(
    query,
    keys,
    values,
    lengths,
    routes,
    gates,
    norm_gain,
    old_holds,
    dup_experts,
    w_gate,
    w_up,
    w_down,
):
    width = lax.axis_size("expert")
    features = norm_gain.shape[0]
    expert_list = lax.iota(jnp.int32, old_holds.shape[0])
    holder = jnp.sum(
        expert_list[:, None] * (old_holds[:, None] == expert_list[None, :]).astype(jnp.int32),
        axis=0,
    )
    doubled = jnp.sum((dup_experts[:, None] == expert_list[None, :]).astype(jnp.int32), axis=0)
    own_gate, own_up, own_down = (w_gate[0], w_up[0], w_down[0])
    attn_one = attend(query[0], keys[0], values[0], lengths[0, 0])
    normed_one = normalize(attn_one, norm_gain)
    flat_one, kept_one = routing(routes[0], jnp.ones_like(doubled), holder, holder, 1)
    packed_one, spot_one = pack(normed_one, flat_one, kept_one, width * CAP)
    received = lax.all_to_all(
        packed_one.reshape(width, CAP // 2, 2, features),
        "expert",
        split_axis=0,
        concat_axis=0,
        tiled=True,
    )
    result = expert_rows(received.reshape(-1, features), own_gate, own_up, own_down)
    back_one = lax.all_to_all(
        result.reshape(received.shape), "expert", split_axis=0, concat_axis=0, tiled=True
    )
    out_one = combine(attn_one, back_one, spot_one, kept_one, gates[0])
    attn_two = attend(query[1], keys[1], values[1], lengths[1, 0])
    normed_two = normalize(attn_two, norm_gain)
    flat_two, kept_two = routing(routes[1], 1 + doubled, holder, holder, 2)
    packed_two, spot_two = pack(normed_two, flat_two, kept_two, width * 2 * CAP)
    received = lax.all_to_all(
        packed_two.reshape(width, 2, CAP, features),
        "expert",
        split_axis=0,
        concat_axis=0,
        tiled=True,
    )
    result = expert_rows(received.reshape(-1, features), own_gate, own_up, own_down).reshape(
        received.shape
    )
    back_two = lax.all_to_all(result, "expert", split_axis=0, concat_axis=0, tiled=True)
    out_two = combine(attn_two, back_two, spot_two, kept_two, gates[1])
    return jnp.stack([out_one, out_two])


def solution(mesh):
    placed = (
        P(None, ("dp", "expert"), None),
        P(None, ("dp", "expert"), None),
        P(None, ("dp", "expert"), None),
        P(None, ("dp", "expert"), None),
        P(None, ("dp", "expert"), None),
        P(None, ("dp", "expert"), None),
        P(),
        P(),
        P(),
        P("expert", None, None),
        P("expert", None, None),
        P("expert", None, None),
    )
    return jax.shard_map(
        shards,
        mesh=mesh,
        in_specs=placed,
        out_specs=P(None, ("dp", "expert"), None),
        check_vma=False,
    )
```

```python
import jax
import jax.numpy as jnp
from jax import lax
from jax.sharding import PartitionSpec as P

HEAD_WIDTH = 128
CAP = 6


def attend(query, key_rows, value_rows, lengths):
    rows = query.shape[0]
    kv_heads = key_rows.shape[1] // HEAD_WIDTH
    query_group = query.shape[1] // HEAD_WIDTH // kv_heads
    ends = jnp.cumsum(lengths)
    position = lax.iota(jnp.int32, rows)
    request = jnp.sum((position[:, None] >= ends[None, :]).astype(jnp.int32), axis=1)
    allowed = (request[:, None] == request[None, :]) & (position[None, :] <= position[:, None])
    query_heads = query.reshape(rows, kv_heads, query_group, HEAD_WIDTH)
    key_heads = key_rows.reshape(rows, kv_heads, HEAD_WIDTH)
    value_heads = value_rows.reshape(rows, kv_heads, HEAD_WIDTH)
    router_logits = jnp.einsum(
        "qhgd,khd->hgqk", query_heads, key_heads, preferred_element_type=jnp.float32
    ) * HEAD_WIDTH ** (-0.5)
    router_logits = jnp.where(allowed[None, None], router_logits, -1e30)
    highest = jnp.max(router_logits, axis=-1, keepdims=True)
    weights = jnp.exp(router_logits - highest)
    probs = (weights / jnp.sum(weights, axis=-1, keepdims=True)).astype(jnp.bfloat16)
    mixed = jnp.einsum("hgqk,khd->qhgd", probs, value_heads, preferred_element_type=jnp.float32)
    return mixed.reshape(rows, kv_heads * query_group * HEAD_WIDTH)


def normalize(attn, gain):
    meansq = jnp.mean(attn * attn, axis=-1, keepdims=True)
    return (attn * lax.rsqrt(meansq + 1e-05) * gain).astype(jnp.bfloat16)


def expert_rows(rows, gate_mat, up_mat, down_mat):
    gate_val = jnp.dot(rows, gate_mat, preferred_element_type=jnp.float32)
    up_val = jnp.dot(rows, up_mat, preferred_element_type=jnp.float32)
    hidden = (jax.nn.silu(gate_val) * up_val).astype(jnp.bfloat16)
    return jnp.dot(hidden, down_mat, preferred_element_type=jnp.float32).astype(jnp.bfloat16)


def routing(routes, copies_of, first_target, second_target, regions):
    expert_list = lax.iota(jnp.int32, copies_of.shape[0])
    hit = (routes[:, :, None] == expert_list[None, None, :]).astype(jnp.int32)
    named = jnp.sum(hit, axis=1)
    before = jnp.cumsum(named, axis=0) - named
    place = jnp.sum(hit * before[:, None, :], axis=2)
    limit = jnp.sum(hit * copies_of[None, None, :], axis=2)
    kept = place < limit * CAP
    which = place // CAP
    target = jnp.where(
        which == 0,
        jnp.sum(hit * first_target[None, None, :], axis=2),
        jnp.sum(hit * second_target[None, None, :], axis=2),
    )
    flat = (target * CAP + place % CAP) * regions + which
    return (flat, kept)


def pack(normed, flat, kept, slots):
    tok_rows = normed.shape[0]
    token = jnp.broadcast_to(lax.iota(jnp.int32, tok_rows)[:, None], flat.shape)
    spot = jnp.where(kept, flat, slots)
    source_row = jnp.full((slots,), tok_rows, jnp.int32).at[spot].set(token, mode="drop")
    padded = jnp.concatenate([normed, jnp.zeros((1, normed.shape[1]), normed.dtype)], axis=0)
    return (padded[source_row], spot)


def combine(attn, returned, spot, kept, gates):
    where = jnp.minimum(spot, returned.size // returned.shape[-1] - 1)
    per_dest = returned.shape[1] * returned.shape[2]
    picked = returned[
        where // per_dest, (where % per_dest) // returned.shape[2], where % returned.shape[2]
    ]
    weight = jnp.where(kept, gates, 0.0)
    mixed = jnp.einsum("tk,tkd->td", weight, picked.astype(jnp.float32))
    return (attn + mixed).astype(jnp.bfloat16)


def shards(
    query,
    keys,
    values,
    lengths,
    routes,
    gates,
    norm_gain,
    old_holds,
    dup_experts,
    w_gate,
    w_up,
    w_down,
):
    width = lax.axis_size("expert")
    features = norm_gain.shape[0]
    expert_list = lax.iota(jnp.int32, old_holds.shape[0])
    holder = jnp.sum(
        expert_list[:, None] * (old_holds[:, None] == expert_list[None, :]).astype(jnp.int32),
        axis=0,
    )
    doubled = jnp.sum((dup_experts[:, None] == expert_list[None, :]).astype(jnp.int32), axis=0)
    own_gate, own_up, own_down = (w_gate[0], w_up[0], w_down[0])
    attn_one = attend(query[0], keys[0], values[0], lengths[0, 0])
    normed_one = normalize(attn_one, norm_gain)
    flat_one, kept_one = routing(routes[0], jnp.ones_like(doubled), holder, holder, 1)
    packed_one, spot_one = pack(normed_one, flat_one, kept_one, width * CAP)
    received = lax.all_to_all(
        packed_one.reshape(width, CAP // 2, 2, features),
        "expert",
        split_axis=0,
        concat_axis=0,
        tiled=True,
    )
    result = expert_rows(received.reshape(-1, features), own_gate, own_up, own_down)
    back_one = lax.all_to_all(
        result.reshape(received.shape), "expert", split_axis=0, concat_axis=0, tiled=True
    )
    out_one = combine(attn_one, back_one, spot_one, kept_one, gates[0])
    attn_two = attend(query[1], keys[1], values[1], lengths[1, 0])
    normed_two = normalize(attn_two, norm_gain)
    flat_two, kept_two = routing(routes[1], 1 + doubled, holder, holder, 2)
    packed_two, spot_two = pack(normed_two, flat_two, kept_two, width * 2 * CAP)
    received = lax.all_to_all(
        packed_two.reshape(width, CAP, 2, features),
        "expert",
        split_axis=0,
        concat_axis=0,
        tiled=True,
    )
    result = expert_rows(received.reshape(-1, features), own_gate, own_up, own_down).reshape(
        received.shape
    )
    back_two = lax.all_to_all(result, "expert", split_axis=0, concat_axis=0, tiled=True)
    out_two = combine(attn_two, back_two, spot_two, kept_two, gates[1])
    return jnp.stack([out_one, out_two])


def solution(mesh):
    placed = (
        P(None, ("dp", "expert"), None),
        P(None, ("dp", "expert"), None),
        P(None, ("dp", "expert"), None),
        P(None, ("dp", "expert"), None),
        P(None, ("dp", "expert"), None),
        P(None, ("dp", "expert"), None),
        P(),
        P(),
        P(),
        P("expert", None, None),
        P("expert", None, None),
        P("expert", None, None),
    )
    return jax.shard_map(
        shards,
        mesh=mesh,
        in_specs=placed,
        out_specs=P(None, ("dp", "expert"), None),
        check_vma=False,
    )
```

```python
import jax
import jax.numpy as jnp
from jax import lax
from jax.sharding import PartitionSpec as P

HEAD_WIDTH = 128
CAP = 6


def attend(query, key_rows, value_rows, lengths):
    rows = query.shape[0]
    kv_heads = key_rows.shape[1] // HEAD_WIDTH
    query_group = query.shape[1] // HEAD_WIDTH // kv_heads
    ends = jnp.cumsum(lengths)
    position = lax.iota(jnp.int32, rows)
    request = jnp.sum((position[:, None] >= ends[None, :]).astype(jnp.int32), axis=1)
    allowed = (request[:, None] == request[None, :]) & (position[None, :] <= position[:, None])
    query_heads = query.reshape(rows, kv_heads, query_group, HEAD_WIDTH)
    key_heads = key_rows.reshape(rows, kv_heads, HEAD_WIDTH)
    value_heads = value_rows.reshape(rows, kv_heads, HEAD_WIDTH)
    router_logits = jnp.einsum(
        "qhgd,khd->hgqk", query_heads, key_heads, preferred_element_type=jnp.float32
    ) * HEAD_WIDTH ** (-0.5)
    router_logits = jnp.where(allowed[None, None], router_logits, -1e30)
    highest = jnp.max(router_logits, axis=-1, keepdims=True)
    weights = jnp.exp(router_logits - highest)
    probs = (weights / jnp.sum(weights, axis=-1, keepdims=True)).astype(jnp.bfloat16)
    mixed = jnp.einsum("hgqk,khd->qhgd", probs, value_heads, preferred_element_type=jnp.float32)
    return mixed.reshape(rows, kv_heads * query_group * HEAD_WIDTH)


def normalize(attn, gain):
    meansq = jnp.mean(attn * attn, axis=-1, keepdims=True)
    return (attn * lax.rsqrt(meansq + 1e-05) * gain).astype(jnp.bfloat16)


def expert_rows(rows, gate_mat, up_mat, down_mat):
    gate_val = jnp.dot(rows, gate_mat, preferred_element_type=jnp.float32)
    up_val = jnp.dot(rows, up_mat, preferred_element_type=jnp.float32)
    hidden = (jax.nn.silu(gate_val) * up_val).astype(jnp.bfloat16)
    return jnp.dot(hidden, down_mat, preferred_element_type=jnp.float32).astype(jnp.bfloat16)


def routing(routes, copies_of, first_target, second_target, regions):
    expert_list = lax.iota(jnp.int32, copies_of.shape[0])
    hit = (routes[:, :, None] == expert_list[None, None, :]).astype(jnp.int32)
    named = jnp.sum(hit, axis=1)
    before = jnp.cumsum(named, axis=0) - named
    place = jnp.sum(hit * before[:, None, :], axis=2)
    limit = jnp.sum(hit * copies_of[None, None, :], axis=2)
    kept = place < limit * CAP
    which = place // CAP
    target = jnp.where(
        which == 0,
        jnp.sum(hit * first_target[None, None, :], axis=2),
        jnp.sum(hit * second_target[None, None, :], axis=2),
    )
    flat = (target * CAP + place % CAP) * regions + which
    return (flat, kept)


def pack(normed, flat, kept, slots):
    tok_rows = normed.shape[0]
    token = jnp.broadcast_to(lax.iota(jnp.int32, tok_rows)[:, None], flat.shape)
    spot = jnp.where(kept, flat, slots)
    source_row = jnp.full((slots,), tok_rows, jnp.int32).at[spot].set(token, mode="drop")
    padded = jnp.concatenate([normed, jnp.zeros((1, normed.shape[1]), normed.dtype)], axis=0)
    return (padded[source_row], spot)


def combine(attn, returned, spot, kept, gates):
    slots = returned.size // returned.shape[-1]
    weight = jnp.where(kept, gates, 0.0)
    onehot = (spot[:, :, None] == lax.iota(jnp.int32, slots)[None, None, :]).astype(jnp.float32)
    spread = jnp.sum(onehot * weight[:, :, None], axis=1).reshape((-1,) + returned.shape[:-1])
    mixed = jnp.einsum(
        "tabc,abcf->tf",
        spread,
        returned.astype(jnp.float32),
        precision=lax.Precision.HIGHEST,
        preferred_element_type=jnp.float32,
    )
    return (attn + mixed).astype(jnp.bfloat16)


def shards(
    query,
    keys,
    values,
    lengths,
    routes,
    gates,
    norm_gain,
    old_holds,
    dup_experts,
    w_gate,
    w_up,
    w_down,
):
    width = lax.axis_size("expert")
    features = norm_gain.shape[0]
    expert_list = lax.iota(jnp.int32, old_holds.shape[0])
    holder = jnp.sum(
        expert_list[:, None] * (old_holds[:, None] == expert_list[None, :]).astype(jnp.int32),
        axis=0,
    )
    doubled = jnp.sum((dup_experts[:, None] == expert_list[None, :]).astype(jnp.int32), axis=0)
    own_gate, own_up, own_down = (w_gate[0], w_up[0], w_down[0])
    attn_one = attend(query[0], keys[0], values[0], lengths[0, 0])
    normed_one = normalize(attn_one, norm_gain)
    flat_one, kept_one = routing(routes[0], jnp.ones_like(doubled), holder, holder, 1)
    packed_one, spot_one = pack(normed_one, flat_one, kept_one, width * CAP)
    received = lax.all_to_all(
        packed_one.reshape(width, CAP // 2, 2, features),
        "expert",
        split_axis=0,
        concat_axis=0,
        tiled=True,
    )
    result = expert_rows(received.reshape(-1, features), own_gate, own_up, own_down)
    back_one = lax.all_to_all(
        result.reshape(received.shape), "expert", split_axis=0, concat_axis=0, tiled=True
    )
    out_one = combine(attn_one, back_one, spot_one, kept_one, gates[0])
    attn_two = attend(query[1], keys[1], values[1], lengths[1, 0])
    normed_two = normalize(attn_two, norm_gain)
    flat_two, kept_two = routing(routes[1], 1 + doubled, holder, holder, 2)
    packed_two, spot_two = pack(normed_two, flat_two, kept_two, width * 2 * CAP)
    received = lax.all_to_all(
        packed_two.reshape(width, CAP, 2, features),
        "expert",
        split_axis=0,
        concat_axis=0,
        tiled=True,
    )
    result = expert_rows(received.reshape(-1, features), own_gate, own_up, own_down).reshape(
        received.shape
    )
    back_two = lax.all_to_all(result, "expert", split_axis=0, concat_axis=0, tiled=True)
    out_two = combine(attn_two, back_two, spot_two, kept_two, gates[1])
    return jnp.stack([out_one, out_two])


def solution(mesh):
    placed = (
        P(None, ("dp", "expert"), None),
        P(None, ("dp", "expert"), None),
        P(None, ("dp", "expert"), None),
        P(None, ("dp", "expert"), None),
        P(None, ("dp", "expert"), None),
        P(None, ("dp", "expert"), None),
        P(),
        P(),
        P(),
        P("expert", None, None),
        P("expert", None, None),
        P("expert", None, None),
    )
    return jax.shard_map(
        shards,
        mesh=mesh,
        in_specs=placed,
        out_specs=P(None, ("dp", "expert"), None),
        check_vma=False,
    )
```

```python
import jax
import jax.numpy as jnp
from jax import lax
from jax.sharding import PartitionSpec as P

HEAD_WIDTH = 128
CAP = 6


def attend(query, key_rows, value_rows, lengths):
    rows = query.shape[0]
    kv_heads = key_rows.shape[1] // HEAD_WIDTH
    query_group = query.shape[1] // HEAD_WIDTH // kv_heads
    ends = jnp.cumsum(lengths)
    position = lax.iota(jnp.int32, rows)
    request = jnp.sum((position[:, None] >= ends[None, :]).astype(jnp.int32), axis=1)
    allowed = (request[:, None] == request[None, :]) & (position[None, :] <= position[:, None])
    query_heads = query.reshape(rows, kv_heads, query_group, HEAD_WIDTH)
    key_heads = key_rows.reshape(rows, kv_heads, HEAD_WIDTH)
    value_heads = value_rows.reshape(rows, kv_heads, HEAD_WIDTH)
    router_logits = jnp.einsum(
        "qhgd,khd->hgqk", query_heads, key_heads, preferred_element_type=jnp.float32
    ) * HEAD_WIDTH ** (-0.5)
    router_logits = jnp.where(allowed[None, None], router_logits, -1e30)
    highest = jnp.max(router_logits, axis=-1, keepdims=True)
    weights = jnp.exp(router_logits - highest)
    probs = (weights / jnp.sum(weights, axis=-1, keepdims=True)).astype(jnp.bfloat16)
    mixed = jnp.einsum("hgqk,khd->qhgd", probs, value_heads, preferred_element_type=jnp.float32)
    return mixed.reshape(rows, kv_heads * query_group * HEAD_WIDTH)


def normalize(attn, gain):
    meansq = jnp.mean(attn * attn, axis=-1, keepdims=True)
    return (attn * lax.rsqrt(meansq + 1e-05) * gain).astype(jnp.bfloat16)


def expert_rows(rows, gate_mat, up_mat, down_mat):
    gate_val = jnp.dot(rows, gate_mat, preferred_element_type=jnp.float32)
    up_val = jnp.dot(rows, up_mat, preferred_element_type=jnp.float32)
    hidden = (jax.nn.silu(gate_val) * up_val).astype(jnp.bfloat16)
    return jnp.dot(hidden, down_mat, preferred_element_type=jnp.float32).astype(jnp.bfloat16)


def routing(routes, copies_of, first_target, second_target, regions):
    expert_list = lax.iota(jnp.int32, copies_of.shape[0])
    hit = (routes[:, :, None] == expert_list[None, None, :]).astype(jnp.int32)
    named = jnp.sum(hit, axis=1)
    before = jnp.cumsum(named, axis=0) - named
    place = jnp.sum(hit * before[:, None, :], axis=2)
    limit = jnp.sum(hit * copies_of[None, None, :], axis=2)
    kept = place < limit * CAP
    which = place // CAP
    target = jnp.where(
        which == 0,
        jnp.sum(hit * first_target[None, None, :], axis=2),
        jnp.sum(hit * second_target[None, None, :], axis=2),
    )
    flat = (target * CAP + place % CAP) * regions + which
    return (flat, kept)


def pack(normed, flat, kept, shape):
    slots = shape[0] * shape[1] * shape[2]
    spot = jnp.where(kept, flat, slots)
    hit = spot[None, :, :] == lax.iota(jnp.int32, slots)[:, None, None]
    picker = jnp.any(hit, axis=2).astype(normed.dtype).reshape(shape + (normed.shape[0],))
    packed = jnp.einsum("abct,tf->abcf", picker, normed, preferred_element_type=jnp.float32)
    return (packed.astype(normed.dtype), spot)


def combine(attn, returned, spot, kept, gates):
    slots = returned.size // returned.shape[-1]
    weight = jnp.where(kept, gates, 0.0)
    onehot = (spot[:, :, None] == lax.iota(jnp.int32, slots)[None, None, :]).astype(jnp.float32)
    spread = jnp.sum(onehot * weight[:, :, None], axis=1).reshape((-1,) + returned.shape[:-1])
    mixed = jnp.einsum(
        "tabc,abcf->tf",
        spread,
        returned.astype(jnp.float32),
        precision=lax.Precision.HIGHEST,
        preferred_element_type=jnp.float32,
    )
    return (attn + mixed).astype(jnp.bfloat16)


def shards(
    query,
    keys,
    values,
    lengths,
    routes,
    gates,
    norm_gain,
    old_holds,
    dup_experts,
    w_gate,
    w_up,
    w_down,
):
    width = lax.axis_size("expert")
    features = norm_gain.shape[0]
    expert_list = lax.iota(jnp.int32, old_holds.shape[0])
    holder = jnp.sum(
        expert_list[:, None] * (old_holds[:, None] == expert_list[None, :]).astype(jnp.int32),
        axis=0,
    )
    doubled = jnp.sum((dup_experts[:, None] == expert_list[None, :]).astype(jnp.int32), axis=0)
    own_gate, own_up, own_down = (w_gate[0], w_up[0], w_down[0])
    attn_one = attend(query[0], keys[0], values[0], lengths[0, 0])
    normed_one = normalize(attn_one, norm_gain)
    flat_one, kept_one = routing(routes[0], jnp.ones_like(doubled), holder, holder, 1)
    packed_one, spot_one = pack(normed_one, flat_one, kept_one, (width, CAP // 2, 2))
    received = lax.all_to_all(
        packed_one,
        "expert",
        split_axis=0,
        concat_axis=0,
        tiled=True,
    )
    result = expert_rows(received.reshape(-1, features), own_gate, own_up, own_down)
    back_one = lax.all_to_all(
        result.reshape(received.shape), "expert", split_axis=0, concat_axis=0, tiled=True
    )
    out_one = combine(attn_one, back_one, spot_one, kept_one, gates[0])
    attn_two = attend(query[1], keys[1], values[1], lengths[1, 0])
    normed_two = normalize(attn_two, norm_gain)
    flat_two, kept_two = routing(routes[1], 1 + doubled, holder, holder, 2)
    packed_two, spot_two = pack(normed_two, flat_two, kept_two, (width, CAP, 2))
    received = lax.all_to_all(
        packed_two,
        "expert",
        split_axis=0,
        concat_axis=0,
        tiled=True,
    )
    result = expert_rows(received.reshape(-1, features), own_gate, own_up, own_down).reshape(
        received.shape
    )
    back_two = lax.all_to_all(result, "expert", split_axis=0, concat_axis=0, tiled=True)
    out_two = combine(attn_two, back_two, spot_two, kept_two, gates[1])
    return jnp.stack([out_one, out_two])


def solution(mesh):
    placed = (
        P(None, ("dp", "expert"), None),
        P(None, ("dp", "expert"), None),
        P(None, ("dp", "expert"), None),
        P(None, ("dp", "expert"), None),
        P(None, ("dp", "expert"), None),
        P(None, ("dp", "expert"), None),
        P(),
        P(),
        P(),
        P("expert", None, None),
        P("expert", None, None),
        P("expert", None, None),
    )
    return jax.shard_map(
        shards,
        mesh=mesh,
        in_specs=placed,
        out_specs=P(None, ("dp", "expert"), None),
        check_vma=False,
    )
```

```python
import jax
import jax.numpy as jnp
from jax import lax
from jax.sharding import PartitionSpec as P

HEAD_WIDTH = 128
CAP = 6


def attend(query, key_rows, value_rows, lengths):
    rows = query.shape[0]
    kv_heads = key_rows.shape[1] // HEAD_WIDTH
    query_group = query.shape[1] // HEAD_WIDTH // kv_heads
    ends = jnp.cumsum(lengths)
    position = lax.iota(jnp.int32, rows)
    request = jnp.sum((position[:, None] >= ends[None, :]).astype(jnp.int32), axis=1)
    allowed = (request[:, None] == request[None, :]) & (position[None, :] <= position[:, None])
    query_heads = query.reshape(rows, kv_heads, query_group, HEAD_WIDTH)
    key_heads = key_rows.reshape(rows, kv_heads, HEAD_WIDTH)
    value_heads = value_rows.reshape(rows, kv_heads, HEAD_WIDTH)
    router_logits = jnp.einsum(
        "qhgd,khd->hgqk", query_heads, key_heads, preferred_element_type=jnp.float32
    ) * HEAD_WIDTH ** (-0.5)
    router_logits = jnp.where(allowed[None, None], router_logits, -1e30)
    highest = jnp.max(router_logits, axis=-1, keepdims=True)
    weights = jnp.exp(router_logits - highest)
    probs = (weights / jnp.sum(weights, axis=-1, keepdims=True)).astype(jnp.bfloat16)
    mixed = jnp.einsum("hgqk,khd->qhgd", probs, value_heads, preferred_element_type=jnp.float32)
    return mixed.reshape(rows, kv_heads * query_group * HEAD_WIDTH)


def normalize(attn, gain):
    meansq = jnp.mean(attn * attn, axis=-1, keepdims=True)
    return (attn * lax.rsqrt(meansq + 1e-05) * gain).astype(jnp.bfloat16)


def expert_rows(rows, gate_mat, up_mat, down_mat):
    gate_val = jnp.dot(rows, gate_mat, preferred_element_type=jnp.float32)
    up_val = jnp.dot(rows, up_mat, preferred_element_type=jnp.float32)
    hidden = (jax.nn.silu(gate_val) * up_val).astype(jnp.bfloat16)
    return jnp.dot(hidden, down_mat, preferred_element_type=jnp.float32).astype(jnp.bfloat16)


def routing(routes, copies_of, first_target, second_target, regions):
    expert_list = lax.iota(jnp.int32, copies_of.shape[0])
    hit = (routes[:, :, None] == expert_list[None, None, :]).astype(jnp.int32)
    named = jnp.sum(hit, axis=1)
    before = jnp.cumsum(named, axis=0) - named
    place = jnp.sum(hit * before[:, None, :], axis=2)
    limit = jnp.sum(hit * copies_of[None, None, :], axis=2)
    kept = place < limit * CAP
    which = place // CAP
    target = jnp.where(
        which == 0,
        jnp.sum(hit * first_target[None, None, :], axis=2),
        jnp.sum(hit * second_target[None, None, :], axis=2),
    )
    flat = (target * CAP + place % CAP) * regions + which
    return (flat, kept)


def pack(normed, flat, kept, shape):
    slots = shape[0] * shape[1] * shape[2]
    spot = jnp.where(kept, flat, slots)
    hit = spot[None, :, :] == lax.iota(jnp.int32, slots)[:, None, None]
    picker = jnp.any(hit, axis=2).astype(normed.dtype).reshape(shape + (normed.shape[0],))
    packed = jnp.einsum("abct,tf->abcf", picker, normed, preferred_element_type=jnp.float32)
    return (packed.astype(normed.dtype), spot)


def gather_pack(normed, flat, kept, shape):
    slots = shape[0] * shape[1] * shape[2]
    tok_rows = normed.shape[0]
    token = jnp.broadcast_to(lax.iota(jnp.int32, tok_rows)[:, None], flat.shape)
    spot = jnp.where(kept, flat, slots)
    source_row = jnp.full((slots,), tok_rows, jnp.int32).at[spot].set(token, mode="drop")
    padded = jnp.concatenate([normed, jnp.zeros((1, normed.shape[1]), normed.dtype)], axis=0)
    return (padded[source_row].reshape(shape + (normed.shape[1],)), spot)


def combine(attn, returned, spot, kept, gates):
    slots = returned.size // returned.shape[-1]
    weight = jnp.where(kept, gates, 0.0)
    onehot = (spot[:, :, None] == lax.iota(jnp.int32, slots)[None, None, :]).astype(jnp.float32)
    spread = jnp.sum(onehot * weight[:, :, None], axis=1).reshape((-1,) + returned.shape[:-1])
    mixed = jnp.einsum(
        "tabc,abcf->tf",
        spread,
        returned.astype(jnp.float32),
        precision=lax.Precision.HIGHEST,
        preferred_element_type=jnp.float32,
    )
    return (attn + mixed).astype(jnp.bfloat16)


def shards(
    query,
    keys,
    values,
    lengths,
    routes,
    gates,
    norm_gain,
    old_holds,
    dup_experts,
    w_gate,
    w_up,
    w_down,
):
    width = lax.axis_size("expert")
    features = norm_gain.shape[0]
    expert_list = lax.iota(jnp.int32, old_holds.shape[0])
    holder = jnp.sum(
        expert_list[:, None] * (old_holds[:, None] == expert_list[None, :]).astype(jnp.int32),
        axis=0,
    )
    doubled = jnp.sum((dup_experts[:, None] == expert_list[None, :]).astype(jnp.int32), axis=0)
    own_gate, own_up, own_down = (w_gate[0], w_up[0], w_down[0])
    attn_one = attend(query[0], keys[0], values[0], lengths[0, 0])
    normed_one = normalize(attn_one, norm_gain)
    flat_one, kept_one = routing(routes[0], jnp.ones_like(doubled), holder, holder, 1)
    packed_one, spot_one = pack(normed_one, flat_one, kept_one, (width, CAP // 2, 2))
    received = lax.all_to_all(
        packed_one,
        "expert",
        split_axis=0,
        concat_axis=0,
        tiled=True,
    )
    result = expert_rows(received.reshape(-1, features), own_gate, own_up, own_down)
    back_one = lax.all_to_all(
        result.reshape(received.shape), "expert", split_axis=0, concat_axis=0, tiled=True
    )
    out_one = combine(attn_one, back_one, spot_one, kept_one, gates[0])
    attn_two = attend(query[1], keys[1], values[1], lengths[1, 0])
    normed_two = normalize(attn_two, norm_gain)
    flat_two, kept_two = routing(routes[1], 1 + doubled, holder, holder, 2)
    packed_two, spot_two = gather_pack(normed_two, flat_two, kept_two, (width, CAP, 2))
    received = lax.all_to_all(
        packed_two,
        "expert",
        split_axis=0,
        concat_axis=0,
        tiled=True,
    )
    result = expert_rows(received.reshape(-1, features), own_gate, own_up, own_down).reshape(
        received.shape
    )
    back_two = lax.all_to_all(result, "expert", split_axis=0, concat_axis=0, tiled=True)
    out_two = combine(attn_two, back_two, spot_two, kept_two, gates[1])
    return jnp.stack([out_one, out_two])


def solution(mesh):
    placed = (
        P(None, ("dp", "expert"), None),
        P(None, ("dp", "expert"), None),
        P(None, ("dp", "expert"), None),
        P(None, ("dp", "expert"), None),
        P(None, ("dp", "expert"), None),
        P(None, ("dp", "expert"), None),
        P(),
        P(),
        P(),
        P("expert", None, None),
        P("expert", None, None),
        P("expert", None, None),
    )
    return jax.shard_map(
        shards,
        mesh=mesh,
        in_specs=placed,
        out_specs=P(None, ("dp", "expert"), None),
        check_vma=False,
    )
```

```python
import jax
import jax.numpy as jnp
from jax import lax
from jax.sharding import PartitionSpec as P
from jax.experimental import pallas as pl
from jax.experimental.pallas import tpu as pltpu

HEAD_WIDTH = 128
CAP = 6


def exchange_kernel(x_ref, o_ref, send_sem, recv_sem, local_sem):
    me = lax.axis_index("expert")
    width = x_ref.shape[0]

    def remote(target, slot):
        return pltpu.make_async_remote_copy(
            src_ref=x_ref.at[target],
            dst_ref=o_ref.at[slot],
            send_sem=send_sem.at[target],
            recv_sem=recv_sem.at[slot],
            device_id={"expert": target},
            device_id_type=pl.DeviceIdType.MESH,
        )

    local = pltpu.make_async_copy(x_ref.at[me], o_ref.at[me], local_sem)
    local.start()

    def start(step, carry):
        remote(lax.rem(me + step, width), me).start()
        return carry

    lax.fori_loop(1, width, start, 0)

    def finish(step, carry):
        remote(lax.rem(me + step, width), me).wait_send()
        remote(me, lax.rem(me + width - step, width)).wait_recv()
        return carry

    lax.fori_loop(1, width, finish, 0)
    local.wait()


def exchange(x):
    width = x.shape[0]
    return pl.pallas_call(
        exchange_kernel,
        out_shape=jax.ShapeDtypeStruct(x.shape, x.dtype),
        in_specs=[pl.BlockSpec(memory_space=pl.ANY)],
        out_specs=pl.BlockSpec(memory_space=pl.ANY),
        scratch_shapes=[
            pltpu.SemaphoreType.DMA((width,)),
            pltpu.SemaphoreType.DMA((width,)),
            pltpu.SemaphoreType.DMA,
        ],
        compiler_params=pltpu.CompilerParams(has_side_effects=True),
    )(x)


def attend(query, key_rows, value_rows, lengths):
    rows = query.shape[0]
    kv_heads = key_rows.shape[1] // HEAD_WIDTH
    query_group = query.shape[1] // HEAD_WIDTH // kv_heads
    ends = jnp.cumsum(lengths)
    position = lax.iota(jnp.int32, rows)
    request = jnp.sum((position[:, None] >= ends[None, :]).astype(jnp.int32), axis=1)
    allowed = (request[:, None] == request[None, :]) & (position[None, :] <= position[:, None])
    query_heads = query.reshape(rows, kv_heads, query_group, HEAD_WIDTH)
    key_heads = key_rows.reshape(rows, kv_heads, HEAD_WIDTH)
    value_heads = value_rows.reshape(rows, kv_heads, HEAD_WIDTH)
    router_logits = jnp.einsum(
        "qhgd,khd->hgqk", query_heads, key_heads, preferred_element_type=jnp.float32
    ) * HEAD_WIDTH ** (-0.5)
    router_logits = jnp.where(allowed[None, None], router_logits, -1e30)
    highest = jnp.max(router_logits, axis=-1, keepdims=True)
    weights = jnp.exp(router_logits - highest)
    probs = (weights / jnp.sum(weights, axis=-1, keepdims=True)).astype(jnp.bfloat16)
    mixed = jnp.einsum("hgqk,khd->qhgd", probs, value_heads, preferred_element_type=jnp.float32)
    return mixed.reshape(rows, kv_heads * query_group * HEAD_WIDTH)


def normalize(attn, gain):
    meansq = jnp.mean(attn * attn, axis=-1, keepdims=True)
    return (attn * lax.rsqrt(meansq + 1e-05) * gain).astype(jnp.bfloat16)


def expert_rows(rows, gate_mat, up_mat, down_mat):
    gate_val = jnp.dot(rows, gate_mat, preferred_element_type=jnp.float32)
    up_val = jnp.dot(rows, up_mat, preferred_element_type=jnp.float32)
    hidden = (jax.nn.silu(gate_val) * up_val).astype(jnp.bfloat16)
    return jnp.dot(hidden, down_mat, preferred_element_type=jnp.float32).astype(jnp.bfloat16)


def routing(routes, copies_of, first_target, second_target, regions):
    expert_list = lax.iota(jnp.int32, copies_of.shape[0])
    hit = (routes[:, :, None] == expert_list[None, None, :]).astype(jnp.int32)
    named = jnp.sum(hit, axis=1)
    before = jnp.cumsum(named, axis=0) - named
    place = jnp.sum(hit * before[:, None, :], axis=2)
    limit = jnp.sum(hit * copies_of[None, None, :], axis=2)
    kept = place < limit * CAP
    which = place // CAP
    target = jnp.where(
        which == 0,
        jnp.sum(hit * first_target[None, None, :], axis=2),
        jnp.sum(hit * second_target[None, None, :], axis=2),
    )
    flat = (target * CAP + place % CAP) * regions + which
    return (flat, kept)


def pack(normed, flat, kept, shape):
    slots = shape[0] * shape[1] * shape[2]
    spot = jnp.where(kept, flat, slots)
    hit = spot[None, :, :] == lax.iota(jnp.int32, slots)[:, None, None]
    picker = jnp.any(hit, axis=2).astype(normed.dtype).reshape(shape + (normed.shape[0],))
    packed = jnp.einsum("abct,tf->abcf", picker, normed, preferred_element_type=jnp.float32)
    return (packed.astype(normed.dtype), spot)


def gather_pack(normed, flat, kept, shape):
    slots = shape[0] * shape[1] * shape[2]
    tok_rows = normed.shape[0]
    token = jnp.broadcast_to(lax.iota(jnp.int32, tok_rows)[:, None], flat.shape)
    spot = jnp.where(kept, flat, slots)
    source_row = jnp.full((slots,), tok_rows, jnp.int32).at[spot].set(token, mode="drop")
    padded = jnp.concatenate([normed, jnp.zeros((1, normed.shape[1]), normed.dtype)], axis=0)
    return (padded[source_row].reshape(shape + (normed.shape[1],)), spot)


def combine(attn, returned, spot, kept, gates):
    slots = returned.size // returned.shape[-1]
    weight = jnp.where(kept, gates, 0.0)
    onehot = (spot[:, :, None] == lax.iota(jnp.int32, slots)[None, None, :]).astype(jnp.float32)
    spread = jnp.sum(onehot * weight[:, :, None], axis=1).reshape((-1,) + returned.shape[:-1])
    mixed = jnp.einsum(
        "tabc,abcf->tf",
        spread,
        returned.astype(jnp.float32),
        precision=lax.Precision.HIGHEST,
        preferred_element_type=jnp.float32,
    )
    return (attn + mixed).astype(jnp.bfloat16)


def shards(
    query,
    keys,
    values,
    lengths,
    routes,
    gates,
    norm_gain,
    old_holds,
    dup_experts,
    w_gate,
    w_up,
    w_down,
):
    width = lax.axis_size("expert")
    features = norm_gain.shape[0]
    expert_list = lax.iota(jnp.int32, old_holds.shape[0])
    holder = jnp.sum(
        expert_list[:, None] * (old_holds[:, None] == expert_list[None, :]).astype(jnp.int32),
        axis=0,
    )
    doubled = jnp.sum((dup_experts[:, None] == expert_list[None, :]).astype(jnp.int32), axis=0)
    own_gate, own_up, own_down = (w_gate[0], w_up[0], w_down[0])
    attn_one = attend(query[0], keys[0], values[0], lengths[0, 0])
    normed_one = normalize(attn_one, norm_gain)
    flat_one, kept_one = routing(routes[0], jnp.ones_like(doubled), holder, holder, 1)
    packed_one, spot_one = pack(normed_one, flat_one, kept_one, (width, CAP // 2, 2))
    received = lax.all_to_all(
        packed_one,
        "expert",
        split_axis=0,
        concat_axis=0,
        tiled=True,
    )
    result = expert_rows(received.reshape(-1, features), own_gate, own_up, own_down)
    back_one = exchange(result.reshape(width, CAP, features)).reshape(width, CAP, 1, features)
    out_one = combine(attn_one, back_one, spot_one, kept_one, gates[0])
    attn_two = attend(query[1], keys[1], values[1], lengths[1, 0])
    normed_two = normalize(attn_two, norm_gain)
    flat_two, kept_two = routing(routes[1], 1 + doubled, holder, holder, 2)
    packed_two, spot_two = gather_pack(normed_two, flat_two, kept_two, (width, CAP, 2))
    received = lax.all_to_all(
        packed_two,
        "expert",
        split_axis=0,
        concat_axis=0,
        tiled=True,
    )
    result = expert_rows(received.reshape(-1, features), own_gate, own_up, own_down).reshape(
        received.shape
    )
    back_two = lax.all_to_all(result, "expert", split_axis=0, concat_axis=0, tiled=True)
    out_two = combine(attn_two, back_two, spot_two, kept_two, gates[1])
    return jnp.stack([out_one, out_two])


def solution(mesh):
    placed = (
        P(None, ("dp", "expert"), None),
        P(None, ("dp", "expert"), None),
        P(None, ("dp", "expert"), None),
        P(None, ("dp", "expert"), None),
        P(None, ("dp", "expert"), None),
        P(None, ("dp", "expert"), None),
        P(),
        P(),
        P(),
        P("expert", None, None),
        P("expert", None, None),
        P("expert", None, None),
    )
    return jax.shard_map(
        shards,
        mesh=mesh,
        in_specs=placed,
        out_specs=P(None, ("dp", "expert"), None),
        check_vma=False,
    )
```

```python
import jax
import jax.numpy as jnp
from jax import lax
from jax.sharding import PartitionSpec as P

HEAD_WIDTH = 128
CAP = 6


def attend(query, key_rows, value_rows, lengths):
    rows = query.shape[0]
    kv_heads = key_rows.shape[1] // HEAD_WIDTH
    query_group = query.shape[1] // HEAD_WIDTH // kv_heads
    ends = jnp.cumsum(lengths)
    position = lax.iota(jnp.int32, rows)
    request = jnp.sum((position[:, None] >= ends[None, :]).astype(jnp.int32), axis=1)
    allowed = (request[:, None] == request[None, :]) & (position[None, :] <= position[:, None])
    query_heads = query.reshape(rows, kv_heads, query_group, HEAD_WIDTH)
    key_heads = key_rows.reshape(rows, kv_heads, HEAD_WIDTH)
    value_heads = value_rows.reshape(rows, kv_heads, HEAD_WIDTH)
    router_logits = jnp.einsum(
        "qhgd,khd->hgqk", query_heads, key_heads, preferred_element_type=jnp.float32
    ) * HEAD_WIDTH ** (-0.5)
    router_logits = jnp.where(allowed[None, None], router_logits, -1e30)
    highest = jnp.max(router_logits, axis=-1, keepdims=True)
    weights = jnp.exp(router_logits - highest)
    probs = (weights / jnp.sum(weights, axis=-1, keepdims=True)).astype(jnp.bfloat16)
    mixed = jnp.einsum("hgqk,khd->qhgd", probs, value_heads, preferred_element_type=jnp.float32)
    return mixed.reshape(rows, kv_heads * query_group * HEAD_WIDTH)


def normalize(attn, gain):
    meansq = jnp.mean(attn * attn, axis=-1, keepdims=True)
    return (attn * lax.rsqrt(meansq + 1e-05) * gain).astype(jnp.bfloat16)


def expert_rows(rows, gate_mat, up_mat, down_mat):
    gate_val = jnp.dot(rows, gate_mat, preferred_element_type=jnp.float32)
    up_val = jnp.dot(rows, up_mat, preferred_element_type=jnp.float32)
    hidden = (jax.nn.silu(gate_val) * up_val).astype(jnp.bfloat16)
    return jnp.dot(hidden, down_mat, preferred_element_type=jnp.float32).astype(jnp.bfloat16)


def routing(routes, copies_of, first_target, second_target, regions):
    expert_list = lax.iota(jnp.int32, copies_of.shape[0])
    hit = (routes[:, :, None] == expert_list[None, None, :]).astype(jnp.int32)
    named = jnp.sum(hit, axis=1)
    before = jnp.cumsum(named, axis=0) - named
    place = jnp.sum(hit * before[:, None, :], axis=2)
    limit = jnp.sum(hit * copies_of[None, None, :], axis=2)
    kept = place < limit * CAP
    which = place // CAP
    target = jnp.where(
        which == 0,
        jnp.sum(hit * first_target[None, None, :], axis=2),
        jnp.sum(hit * second_target[None, None, :], axis=2),
    )
    flat = (target * CAP + place % CAP) * regions + which
    return (flat, kept)


def pack(normed, flat, kept, shape):
    slots = shape[0] * shape[1] * shape[2]
    spot = jnp.where(kept, flat, slots)
    hit = spot[None, :, :] == lax.iota(jnp.int32, slots)[:, None, None]
    picker = jnp.any(hit, axis=2).astype(normed.dtype).reshape(shape + (normed.shape[0],))
    packed = jnp.einsum("abct,tf->abcf", picker, normed, preferred_element_type=jnp.float32)
    return (packed.astype(normed.dtype), spot)


def gather_pack(normed, flat, kept, shape):
    slots = shape[0] * shape[1] * shape[2]
    tok_rows = normed.shape[0]
    token = jnp.broadcast_to(lax.iota(jnp.int32, tok_rows)[:, None], flat.shape)
    spot = jnp.where(kept, flat, slots)
    source_row = jnp.full((slots,), tok_rows, jnp.int32).at[spot].set(token, mode="drop")
    padded = jnp.concatenate([normed, jnp.zeros((1, normed.shape[1]), normed.dtype)], axis=0)
    return (padded[source_row].reshape(shape + (normed.shape[1],)), spot)


def combine(attn, returned, spot, kept, gates):
    slots = returned.size // returned.shape[-1]
    weight = jnp.where(kept, gates, 0.0)
    onehot = (spot[:, :, None] == lax.iota(jnp.int32, slots)[None, None, :]).astype(jnp.float32)
    spread = jnp.sum(onehot * weight[:, :, None], axis=1).reshape((-1,) + returned.shape[:-1])
    mixed = jnp.einsum(
        "tabc,abcf->tf",
        spread,
        returned.astype(jnp.float32),
        precision=lax.Precision.HIGHEST,
        preferred_element_type=jnp.float32,
    )
    return (attn + mixed).astype(jnp.bfloat16)


def shards(
    query,
    keys,
    values,
    lengths,
    routes,
    gates,
    norm_gain,
    old_holds,
    dup_experts,
    w_gate,
    w_up,
    w_down,
):
    width = lax.axis_size("expert")
    features = norm_gain.shape[0]
    expert_list = lax.iota(jnp.int32, old_holds.shape[0])
    holder = jnp.sum(
        expert_list[:, None] * (old_holds[:, None] == expert_list[None, :]).astype(jnp.int32),
        axis=0,
    )
    doubled = jnp.sum((dup_experts[:, None] == expert_list[None, :]).astype(jnp.int32), axis=0)
    own_gate, own_up, own_down = (w_gate[0], w_up[0], w_down[0])
    attn_one = attend(query[0], keys[0], values[0], lengths[0, 0])
    attn_two = attend(query[1], keys[1], values[1], lengths[1, 0])
    normed_one = normalize(attn_one, norm_gain)
    normed_two = normalize(attn_two, norm_gain)
    flat_one, kept_one = routing(routes[0], jnp.ones_like(doubled), holder, holder, 1)
    flat_two, kept_two = routing(routes[1], 1 + doubled, holder, holder, 2)
    per_dest = 3 * CAP
    slots = width * per_dest
    spot_one = jnp.where(kept_one, flat_one, width * CAP)
    spot_two = jnp.where(kept_two, flat_two, width * 2 * CAP)
    merged_one = jnp.where(kept_one, (flat_one // CAP) * per_dest + flat_one % CAP, slots)
    merged_two = jnp.where(
        kept_two, (flat_two // (2 * CAP)) * per_dest + CAP + flat_two % (2 * CAP), slots
    )
    slot_list = lax.iota(jnp.int32, slots)[:, None, None]
    picker = jnp.concatenate(
        [
            jnp.any(merged_one[None, :, :] == slot_list, axis=2),
            jnp.any(merged_two[None, :, :] == slot_list, axis=2),
        ],
        axis=1,
    ).astype(normed_one.dtype)
    normed = jnp.concatenate([normed_one, normed_two], axis=0)
    packed = jnp.einsum(
        "abct,tf->abcf",
        picker.reshape(width, per_dest // 2, 2, -1),
        normed,
        preferred_element_type=jnp.float32,
    ).astype(normed.dtype)
    received = lax.all_to_all(packed, "expert", split_axis=0, concat_axis=0, tiled=True)
    received_one = received[:, : CAP // 2]
    received_two = received[:, CAP // 2 :]
    result = expert_rows(received_one.reshape(-1, features), own_gate, own_up, own_down)
    back_one = lax.all_to_all(
        result.reshape(received_one.shape), "expert", split_axis=0, concat_axis=0, tiled=True
    )
    out_one = combine(attn_one, back_one, spot_one, kept_one, gates[0])
    result = expert_rows(received_two.reshape(-1, features), own_gate, own_up, own_down).reshape(
        received_two.shape
    )
    back_two = lax.all_to_all(result, "expert", split_axis=0, concat_axis=0, tiled=True)
    out_two = combine(attn_two, back_two, spot_two, kept_two, gates[1])
    return jnp.stack([out_one, out_two])


def solution(mesh):
    placed = (
        P(None, ("dp", "expert"), None),
        P(None, ("dp", "expert"), None),
        P(None, ("dp", "expert"), None),
        P(None, ("dp", "expert"), None),
        P(None, ("dp", "expert"), None),
        P(None, ("dp", "expert"), None),
        P(),
        P(),
        P(),
        P("expert", None, None),
        P("expert", None, None),
        P("expert", None, None),
    )
    return jax.shard_map(
        shards,
        mesh=mesh,
        in_specs=placed,
        out_specs=P(None, ("dp", "expert"), None),
        check_vma=False,
    )
```

```python
import jax
import jax.numpy as jnp
from jax import lax
from jax.sharding import PartitionSpec as P
from jax.experimental import pallas as pl
from jax.experimental.pallas import tpu as pltpu

HEAD_WIDTH = 128
CAP = 6


def attend(query, key_rows, value_rows, lengths):
    rows = query.shape[0]
    kv_heads = key_rows.shape[1] // HEAD_WIDTH
    query_group = query.shape[1] // HEAD_WIDTH // kv_heads
    ends = jnp.cumsum(lengths)
    position = lax.iota(jnp.int32, rows)
    request = jnp.sum((position[:, None] >= ends[None, :]).astype(jnp.int32), axis=1)
    allowed = (request[:, None] == request[None, :]) & (position[None, :] <= position[:, None])
    query_heads = query.reshape(rows, kv_heads, query_group, HEAD_WIDTH)
    key_heads = key_rows.reshape(rows, kv_heads, HEAD_WIDTH)
    value_heads = value_rows.reshape(rows, kv_heads, HEAD_WIDTH)
    router_logits = jnp.einsum(
        "qhgd,khd->hgqk", query_heads, key_heads, preferred_element_type=jnp.float32
    ) * HEAD_WIDTH ** (-0.5)
    router_logits = jnp.where(allowed[None, None], router_logits, -1e30)
    highest = jnp.max(router_logits, axis=-1, keepdims=True)
    weights = jnp.exp(router_logits - highest)
    probs = (weights / jnp.sum(weights, axis=-1, keepdims=True)).astype(jnp.bfloat16)
    mixed = jnp.einsum("hgqk,khd->qhgd", probs, value_heads, preferred_element_type=jnp.float32)
    return mixed.reshape(rows, kv_heads * query_group * HEAD_WIDTH)


def attend_kernel(query_ref, key_ref, value_ref, ends_ref, gain_ref, attn_ref, normed_ref):
    rows = query_ref.shape[0]
    kv_heads = key_ref.shape[1] // HEAD_WIDTH
    query_group = query_ref.shape[1] // HEAD_WIDTH // kv_heads
    ends = ends_ref[...]
    position = lax.broadcasted_iota(jnp.int32, (rows, ends.shape[1]), 0)
    request = jnp.sum((position >= ends).astype(jnp.int32), axis=1, keepdims=True)
    row = lax.broadcasted_iota(jnp.int32, (rows, rows), 0)
    col = lax.broadcasted_iota(jnp.int32, (rows, rows), 1)
    request_col = jnp.sum(
        (lax.broadcasted_iota(jnp.int32, (ends.shape[1], rows), 1) >= ends.reshape(-1, 1)).astype(
            jnp.int32
        ),
        axis=0,
        keepdims=True,
    )
    allowed = (request == request_col) & (col <= row)
    for head in range(kv_heads * query_group):
        kv = head // query_group
        q = query_ref[:, head * HEAD_WIDTH : (head + 1) * HEAD_WIDTH]
        k = key_ref[:, kv * HEAD_WIDTH : (kv + 1) * HEAD_WIDTH]
        v = value_ref[:, kv * HEAD_WIDTH : (kv + 1) * HEAD_WIDTH]
        logits = lax.dot_general(
            q, k, (((1,), (1,)), ((), ())), preferred_element_type=jnp.float32
        ) * HEAD_WIDTH ** (-0.5)
        logits = jnp.where(allowed, logits, -1e30)
        highest = jnp.max(logits, axis=-1, keepdims=True)
        weights = jnp.exp(logits - highest)
        probs = (weights / jnp.sum(weights, axis=-1, keepdims=True)).astype(jnp.bfloat16)
        attn_ref[:, head * HEAD_WIDTH : (head + 1) * HEAD_WIDTH] = jnp.dot(
            probs, v, preferred_element_type=jnp.float32
        )
    attn = attn_ref[...]
    meansq = jnp.mean(attn * attn, axis=-1, keepdims=True)
    normed_ref[...] = (attn * lax.rsqrt(meansq + 1e-05) * gain_ref[...]).astype(jnp.bfloat16)


def attend_normed(query, key_rows, value_rows, lengths, gain):
    rows, features = query.shape
    ends = jnp.cumsum(lengths).reshape(1, -1)
    vmem = pl.BlockSpec(memory_space=pltpu.VMEM)
    return pl.pallas_call(
        attend_kernel,
        out_shape=(
            jax.ShapeDtypeStruct((rows, features), jnp.float32),
            jax.ShapeDtypeStruct((rows, features), jnp.bfloat16),
        ),
        in_specs=[vmem] * 5,
        out_specs=(vmem, vmem),
    )(query, key_rows, value_rows, ends, gain.reshape(1, -1))


def normalize(attn, gain):
    meansq = jnp.mean(attn * attn, axis=-1, keepdims=True)
    return (attn * lax.rsqrt(meansq + 1e-05) * gain).astype(jnp.bfloat16)


def expert_rows(rows, gate_mat, up_mat, down_mat):
    gate_val = jnp.dot(rows, gate_mat, preferred_element_type=jnp.float32)
    up_val = jnp.dot(rows, up_mat, preferred_element_type=jnp.float32)
    hidden = (jax.nn.silu(gate_val) * up_val).astype(jnp.bfloat16)
    return jnp.dot(hidden, down_mat, preferred_element_type=jnp.float32).astype(jnp.bfloat16)


def routing(routes, copies_of, first_target, second_target, regions):
    expert_list = lax.iota(jnp.int32, copies_of.shape[0])
    hit = (routes[:, :, None] == expert_list[None, None, :]).astype(jnp.int32)
    named = jnp.sum(hit, axis=1)
    before = jnp.cumsum(named, axis=0) - named
    place = jnp.sum(hit * before[:, None, :], axis=2)
    limit = jnp.sum(hit * copies_of[None, None, :], axis=2)
    kept = place < limit * CAP
    which = place // CAP
    target = jnp.where(
        which == 0,
        jnp.sum(hit * first_target[None, None, :], axis=2),
        jnp.sum(hit * second_target[None, None, :], axis=2),
    )
    flat = (target * CAP + place % CAP) * regions + which
    return (flat, kept)


def pack(normed, flat, kept, shape):
    slots = shape[0] * shape[1] * shape[2]
    spot = jnp.where(kept, flat, slots)
    hit = spot[None, :, :] == lax.iota(jnp.int32, slots)[:, None, None]
    picker = jnp.any(hit, axis=2).astype(normed.dtype).reshape(shape + (normed.shape[0],))
    packed = jnp.einsum("abct,tf->abcf", picker, normed, preferred_element_type=jnp.float32)
    return (packed.astype(normed.dtype), spot)


def gather_pack(normed, flat, kept, shape):
    slots = shape[0] * shape[1] * shape[2]
    tok_rows = normed.shape[0]
    token = jnp.broadcast_to(lax.iota(jnp.int32, tok_rows)[:, None], flat.shape)
    spot = jnp.where(kept, flat, slots)
    source_row = jnp.full((slots,), tok_rows, jnp.int32).at[spot].set(token, mode="drop")
    padded = jnp.concatenate([normed, jnp.zeros((1, normed.shape[1]), normed.dtype)], axis=0)
    return (padded[source_row].reshape(shape + (normed.shape[1],)), spot)


def combine(attn, returned, spot, kept, gates):
    slots = returned.size // returned.shape[-1]
    weight = jnp.where(kept, gates, 0.0)
    onehot = (spot[:, :, None] == lax.iota(jnp.int32, slots)[None, None, :]).astype(jnp.float32)
    spread = jnp.sum(onehot * weight[:, :, None], axis=1).reshape((-1,) + returned.shape[:-1])
    mixed = jnp.einsum(
        "tabc,abcf->tf",
        spread,
        returned.astype(jnp.float32),
        precision=lax.Precision.HIGHEST,
        preferred_element_type=jnp.float32,
    )
    return (attn + mixed).astype(jnp.bfloat16)


def shards(
    query,
    keys,
    values,
    lengths,
    routes,
    gates,
    norm_gain,
    old_holds,
    dup_experts,
    w_gate,
    w_up,
    w_down,
):
    width = lax.axis_size("expert")
    features = norm_gain.shape[0]
    expert_list = lax.iota(jnp.int32, old_holds.shape[0])
    holder = jnp.sum(
        expert_list[:, None] * (old_holds[:, None] == expert_list[None, :]).astype(jnp.int32),
        axis=0,
    )
    doubled = jnp.sum((dup_experts[:, None] == expert_list[None, :]).astype(jnp.int32), axis=0)
    own_gate, own_up, own_down = (w_gate[0], w_up[0], w_down[0])
    attn_one, normed_one = attend_normed(query[0], keys[0], values[0], lengths[0, 0], norm_gain)
    flat_one, kept_one = routing(routes[0], jnp.ones_like(doubled), holder, holder, 1)
    packed_one, spot_one = pack(normed_one, flat_one, kept_one, (width, CAP // 2, 2))
    received = lax.all_to_all(
        packed_one,
        "expert",
        split_axis=0,
        concat_axis=0,
        tiled=True,
    )
    result = expert_rows(received.reshape(-1, features), own_gate, own_up, own_down)
    back_one = lax.all_to_all(
        result.reshape(received.shape), "expert", split_axis=0, concat_axis=0, tiled=True
    )
    out_one = combine(attn_one, back_one, spot_one, kept_one, gates[0])
    attn_two, normed_two = attend_normed(query[1], keys[1], values[1], lengths[1, 0], norm_gain)
    flat_two, kept_two = routing(routes[1], 1 + doubled, holder, holder, 2)
    packed_two, spot_two = gather_pack(normed_two, flat_two, kept_two, (width, CAP, 2))
    received = lax.all_to_all(
        packed_two,
        "expert",
        split_axis=0,
        concat_axis=0,
        tiled=True,
    )
    result = expert_rows(received.reshape(-1, features), own_gate, own_up, own_down).reshape(
        received.shape
    )
    back_two = lax.all_to_all(result, "expert", split_axis=0, concat_axis=0, tiled=True)
    out_two = combine(attn_two, back_two, spot_two, kept_two, gates[1])
    return jnp.stack([out_one, out_two])


def solution(mesh):
    placed = (
        P(None, ("dp", "expert"), None),
        P(None, ("dp", "expert"), None),
        P(None, ("dp", "expert"), None),
        P(None, ("dp", "expert"), None),
        P(None, ("dp", "expert"), None),
        P(None, ("dp", "expert"), None),
        P(),
        P(),
        P(),
        P("expert", None, None),
        P("expert", None, None),
        P("expert", None, None),
    )
    return jax.shard_map(
        shards,
        mesh=mesh,
        in_specs=placed,
        out_specs=P(None, ("dp", "expert"), None),
        check_vma=False,
    )
```

```python
import jax
import jax.numpy as jnp
from jax import lax
from jax.sharding import PartitionSpec as P
from jax.experimental import pallas as pl
from jax.experimental.pallas import tpu as pltpu

HEAD_WIDTH = 128
CAP = 6


def attend(query, key_rows, value_rows, lengths):
    rows = query.shape[0]
    kv_heads = key_rows.shape[1] // HEAD_WIDTH
    query_group = query.shape[1] // HEAD_WIDTH // kv_heads
    ends = jnp.cumsum(lengths)
    position = lax.iota(jnp.int32, rows)
    request = jnp.sum((position[:, None] >= ends[None, :]).astype(jnp.int32), axis=1)
    allowed = (request[:, None] == request[None, :]) & (position[None, :] <= position[:, None])
    query_heads = query.reshape(rows, kv_heads, query_group, HEAD_WIDTH)
    key_heads = key_rows.reshape(rows, kv_heads, HEAD_WIDTH)
    value_heads = value_rows.reshape(rows, kv_heads, HEAD_WIDTH)
    router_logits = jnp.einsum(
        "qhgd,khd->hgqk", query_heads, key_heads, preferred_element_type=jnp.float32
    ) * HEAD_WIDTH ** (-0.5)
    router_logits = jnp.where(allowed[None, None], router_logits, -1e30)
    highest = jnp.max(router_logits, axis=-1, keepdims=True)
    weights = jnp.exp(router_logits - highest)
    probs = (weights / jnp.sum(weights, axis=-1, keepdims=True)).astype(jnp.bfloat16)
    mixed = jnp.einsum("hgqk,khd->qhgd", probs, value_heads, preferred_element_type=jnp.float32)
    return mixed.reshape(rows, kv_heads * query_group * HEAD_WIDTH)


def attend_kernel(query_ref, key_ref, value_ref, ends_ref, gain_ref, attn_ref, normed_ref):
    rows = query_ref.shape[0]
    kv_heads = key_ref.shape[1] // HEAD_WIDTH
    group = query_ref.shape[1] // HEAD_WIDTH // kv_heads
    ends = ends_ref[...]
    position = lax.broadcasted_iota(jnp.int32, (rows, ends.shape[1]), 0)
    request = jnp.sum((position >= ends).astype(jnp.int32), axis=1, keepdims=True)
    request_col = jnp.sum(
        (lax.broadcasted_iota(jnp.int32, (ends.shape[1], rows), 1) >= ends.reshape(-1, 1)).astype(
            jnp.int32
        ),
        axis=0,
        keepdims=True,
    )
    row = lax.broadcasted_iota(jnp.int32, (rows, rows), 0)
    col = lax.broadcasted_iota(jnp.int32, (rows, rows), 1)
    allowed = (request == request_col) & (col <= row)
    allowed = jnp.concatenate([allowed] * group, axis=0)
    for kv in range(kv_heads):
        q = jnp.concatenate(
            [
                query_ref[:, (kv * group + g) * HEAD_WIDTH : (kv * group + g + 1) * HEAD_WIDTH]
                for g in range(group)
            ],
            axis=0,
        )
        k = key_ref[:, kv * HEAD_WIDTH : (kv + 1) * HEAD_WIDTH]
        v = value_ref[:, kv * HEAD_WIDTH : (kv + 1) * HEAD_WIDTH]
        logits = lax.dot_general(
            q, k, (((1,), (1,)), ((), ())), preferred_element_type=jnp.float32
        ) * HEAD_WIDTH ** (-0.5)
        logits = jnp.where(allowed, logits, -1e30)
        highest = jnp.max(logits, axis=-1, keepdims=True)
        weights = jnp.exp(logits - highest)
        probs = (weights / jnp.sum(weights, axis=-1, keepdims=True)).astype(jnp.bfloat16)
        mixed = jnp.dot(probs, v, preferred_element_type=jnp.float32)
        for g in range(group):
            head = kv * group + g
            attn_ref[:, head * HEAD_WIDTH : (head + 1) * HEAD_WIDTH] = mixed[g * rows : (g + 1) * rows]
    attn = attn_ref[...]
    meansq = jnp.mean(attn * attn, axis=-1, keepdims=True)
    normed_ref[...] = (attn * lax.rsqrt(meansq + 1e-05) * gain_ref[...]).astype(jnp.bfloat16)


def attend_normed(batch, query, key_rows, value_rows, lengths, gain):
    rows, features = query.shape[1:]
    ends = jnp.cumsum(lengths, axis=-1)

    def pick(array):
        return pl.BlockSpec((None,) + array.shape[1:], lambda i: (batch, 0, 0))

    return pl.pallas_call(
        attend_kernel,
        grid=(1,),
        out_shape=(
            jax.ShapeDtypeStruct((rows, features), jnp.float32),
            jax.ShapeDtypeStruct((rows, features), jnp.bfloat16),
        ),
        in_specs=[
            pick(query),
            pick(key_rows),
            pick(value_rows),
            pick(ends),
            pl.BlockSpec((1, features), lambda i: (0, 0)),
        ],
        out_specs=(
            pl.BlockSpec((rows, features), lambda i: (0, 0)),
            pl.BlockSpec((rows, features), lambda i: (0, 0)),
        ),
    )(query, key_rows, value_rows, ends, gain.reshape(1, -1))


def normalize(attn, gain):
    meansq = jnp.mean(attn * attn, axis=-1, keepdims=True)
    return (attn * lax.rsqrt(meansq + 1e-05) * gain).astype(jnp.bfloat16)


def expert_rows(rows, gate_mat, up_mat, down_mat):
    gate_val = jnp.dot(rows, gate_mat, preferred_element_type=jnp.float32)
    up_val = jnp.dot(rows, up_mat, preferred_element_type=jnp.float32)
    hidden = (jax.nn.silu(gate_val) * up_val).astype(jnp.bfloat16)
    return jnp.dot(hidden, down_mat, preferred_element_type=jnp.float32).astype(jnp.bfloat16)


def routing(routes, copies_of, first_target, second_target, regions):
    expert_list = lax.iota(jnp.int32, copies_of.shape[0])
    hit = (routes[:, :, None] == expert_list[None, None, :]).astype(jnp.int32)
    named = jnp.sum(hit, axis=1)
    before = jnp.cumsum(named, axis=0) - named
    place = jnp.sum(hit * before[:, None, :], axis=2)
    limit = jnp.sum(hit * copies_of[None, None, :], axis=2)
    kept = place < limit * CAP
    which = place // CAP
    target = jnp.where(
        which == 0,
        jnp.sum(hit * first_target[None, None, :], axis=2),
        jnp.sum(hit * second_target[None, None, :], axis=2),
    )
    flat = (target * CAP + place % CAP) * regions + which
    return (flat, kept)


def pack(normed, flat, kept, shape):
    slots = shape[0] * shape[1] * shape[2]
    spot = jnp.where(kept, flat, slots)
    hit = spot[None, :, :] == lax.iota(jnp.int32, slots)[:, None, None]
    picker = jnp.any(hit, axis=2).astype(normed.dtype).reshape(shape + (normed.shape[0],))
    packed = jnp.einsum("abct,tf->abcf", picker, normed, preferred_element_type=jnp.float32)
    return (packed.astype(normed.dtype), spot)


def gather_pack(normed, flat, kept, shape):
    slots = shape[0] * shape[1] * shape[2]
    tok_rows = normed.shape[0]
    token = jnp.broadcast_to(lax.iota(jnp.int32, tok_rows)[:, None], flat.shape)
    spot = jnp.where(kept, flat, slots)
    source_row = jnp.full((slots,), tok_rows, jnp.int32).at[spot].set(token, mode="drop")
    padded = jnp.concatenate([normed, jnp.zeros((1, normed.shape[1]), normed.dtype)], axis=0)
    return (padded[source_row].reshape(shape + (normed.shape[1],)), spot)


def combine(attn, returned, spot, kept, gates):
    slots = returned.size // returned.shape[-1]
    weight = jnp.where(kept, gates, 0.0)
    onehot = (spot[:, :, None] == lax.iota(jnp.int32, slots)[None, None, :]).astype(jnp.float32)
    spread = jnp.sum(onehot * weight[:, :, None], axis=1).reshape((-1,) + returned.shape[:-1])
    mixed = jnp.einsum(
        "tabc,abcf->tf",
        spread,
        returned.astype(jnp.float32),
        precision=lax.Precision.HIGHEST,
        preferred_element_type=jnp.float32,
    )
    return (attn + mixed).astype(jnp.bfloat16)


def shards(
    query,
    keys,
    values,
    lengths,
    routes,
    gates,
    norm_gain,
    old_holds,
    dup_experts,
    w_gate,
    w_up,
    w_down,
):
    width = lax.axis_size("expert")
    features = norm_gain.shape[0]
    expert_list = lax.iota(jnp.int32, old_holds.shape[0])
    holder = jnp.sum(
        expert_list[:, None] * (old_holds[:, None] == expert_list[None, :]).astype(jnp.int32),
        axis=0,
    )
    doubled = jnp.sum((dup_experts[:, None] == expert_list[None, :]).astype(jnp.int32), axis=0)
    own_gate, own_up, own_down = (w_gate[0], w_up[0], w_down[0])
    attn_one, normed_one = attend_normed(0, query, keys, values, lengths, norm_gain)
    flat_one, kept_one = routing(routes[0], jnp.ones_like(doubled), holder, holder, 1)
    packed_one, spot_one = pack(normed_one, flat_one, kept_one, (width, CAP // 2, 2))
    received = lax.all_to_all(
        packed_one,
        "expert",
        split_axis=0,
        concat_axis=0,
        tiled=True,
    )
    result = expert_rows(received.reshape(-1, features), own_gate, own_up, own_down)
    back_one = lax.all_to_all(
        result.reshape(received.shape), "expert", split_axis=0, concat_axis=0, tiled=True
    )
    out_one = combine(attn_one, back_one, spot_one, kept_one, gates[0])
    attn_two, normed_two = attend_normed(1, query, keys, values, lengths, norm_gain)
    flat_two, kept_two = routing(routes[1], 1 + doubled, holder, holder, 2)
    packed_two, spot_two = gather_pack(normed_two, flat_two, kept_two, (width, CAP, 2))
    received = lax.all_to_all(
        packed_two,
        "expert",
        split_axis=0,
        concat_axis=0,
        tiled=True,
    )
    result = expert_rows(received.reshape(-1, features), own_gate, own_up, own_down).reshape(
        received.shape
    )
    back_two = lax.all_to_all(result, "expert", split_axis=0, concat_axis=0, tiled=True)
    out_two = combine(attn_two, back_two, spot_two, kept_two, gates[1])
    return jnp.stack([out_one, out_two])


def solution(mesh):
    placed = (
        P(None, ("dp", "expert"), None),
        P(None, ("dp", "expert"), None),
        P(None, ("dp", "expert"), None),
        P(None, ("dp", "expert"), None),
        P(None, ("dp", "expert"), None),
        P(None, ("dp", "expert"), None),
        P(),
        P(),
        P(),
        P("expert", None, None),
        P("expert", None, None),
        P("expert", None, None),
    )
    return jax.shard_map(
        shards,
        mesh=mesh,
        in_specs=placed,
        out_specs=P(None, ("dp", "expert"), None),
        check_vma=False,
    )
```

```python
import jax
import jax.numpy as jnp
from jax import lax
from jax.sharding import PartitionSpec as P

HEAD_WIDTH = 128
CAP = 6


def attend(query, key_rows, value_rows, lengths):
    rows = query.shape[0]
    kv_heads = key_rows.shape[1] // HEAD_WIDTH
    query_group = query.shape[1] // HEAD_WIDTH // kv_heads
    ends = jnp.cumsum(lengths)
    position = lax.iota(jnp.int32, rows)
    request = jnp.sum((position[:, None] >= ends[None, :]).astype(jnp.int32), axis=1)
    allowed = (request[:, None] == request[None, :]) & (position[None, :] <= position[:, None])
    query_heads = query.reshape(rows, kv_heads, query_group, HEAD_WIDTH)
    key_heads = key_rows.reshape(rows, kv_heads, HEAD_WIDTH)
    value_heads = value_rows.reshape(rows, kv_heads, HEAD_WIDTH)
    router_logits = jnp.einsum(
        "qhgd,khd->hgqk", query_heads, key_heads, preferred_element_type=jnp.float32
    ) * HEAD_WIDTH ** (-0.5)
    router_logits = jnp.where(allowed[None, None], router_logits, -1e30)
    highest = jnp.max(router_logits, axis=-1, keepdims=True)
    weights = jnp.exp(router_logits - highest)
    probs = (weights / jnp.sum(weights, axis=-1, keepdims=True)).astype(jnp.bfloat16)
    mixed = jnp.einsum("hgqk,khd->qhgd", probs, value_heads, preferred_element_type=jnp.float32)
    return mixed.reshape(rows, kv_heads * query_group * HEAD_WIDTH)


def normalize(attn, gain):
    meansq = jnp.mean(attn * attn, axis=-1, keepdims=True)
    return (attn * lax.rsqrt(meansq + 1e-05) * gain).astype(jnp.bfloat16)


def expert_rows(rows, gate_mat, up_mat, down_mat):
    gate_val = jnp.dot(rows, gate_mat, preferred_element_type=jnp.float32)
    up_val = jnp.dot(rows, up_mat, preferred_element_type=jnp.float32)
    hidden = (jax.nn.silu(gate_val) * up_val).astype(jnp.bfloat16)
    return jnp.dot(hidden, down_mat, preferred_element_type=jnp.float32).astype(jnp.bfloat16)


def routing(routes, copies_of, first_target, second_target, regions):
    expert_list = lax.iota(jnp.int32, copies_of.shape[0])
    hit = (routes[:, :, None] == expert_list[None, None, :]).astype(jnp.int32)
    named = jnp.sum(hit, axis=1)
    before = jnp.cumsum(named, axis=0) - named
    place = jnp.sum(hit * before[:, None, :], axis=2)
    limit = jnp.sum(hit * copies_of[None, None, :], axis=2)
    kept = place < limit * CAP
    which = place // CAP
    target = jnp.where(
        which == 0,
        jnp.sum(hit * first_target[None, None, :], axis=2),
        jnp.sum(hit * second_target[None, None, :], axis=2),
    )
    flat = (target * CAP + place % CAP) * regions + which
    return (flat, kept)


def pack(normed, flat, kept, shape):
    slots = shape[0] * shape[1] * shape[2]
    spot = jnp.where(kept, flat, slots)
    hit = spot[None, :, :] == lax.iota(jnp.int32, slots)[:, None, None]
    picker = jnp.any(hit, axis=2).astype(normed.dtype).reshape(shape + (normed.shape[0],))
    packed = jnp.einsum("abct,tf->abcf", picker, normed, preferred_element_type=jnp.float32)
    return (packed.astype(normed.dtype), spot)


def gather_pack(normed, flat, kept, shape):
    slots = shape[0] * shape[1] * shape[2]
    tok_rows = normed.shape[0]
    token = jnp.broadcast_to(lax.iota(jnp.int32, tok_rows)[:, None], flat.shape)
    spot = jnp.where(kept, flat, slots)
    source_row = jnp.full((slots,), tok_rows, jnp.int32).at[spot].set(token, mode="drop")
    padded = jnp.concatenate([normed, jnp.zeros((1, normed.shape[1]), normed.dtype)], axis=0)
    return (padded[source_row].reshape(shape + (normed.shape[1],)), spot)


def combine(attn, returned, spot, kept, gates, split=False):
    slots = returned.size // returned.shape[-1]
    weight = jnp.where(kept, gates, 0.0)
    onehot = (spot[:, :, None] == lax.iota(jnp.int32, slots)[None, None, :]).astype(jnp.float32)
    spread = jnp.sum(onehot * weight[:, :, None], axis=1).reshape((-1,) + returned.shape[:-1])
    if split:
        high = spread.astype(returned.dtype)
        rest = spread - high.astype(jnp.float32)
        middle = rest.astype(returned.dtype)
        mixed = sum(
            jnp.einsum("tabc,abcf->tf", part, returned, preferred_element_type=jnp.float32)
            for part in (high, middle)
        )
    else:
        mixed = jnp.einsum(
            "tabc,abcf->tf",
            spread,
            returned.astype(jnp.float32),
            precision=lax.Precision.HIGHEST,
            preferred_element_type=jnp.float32,
        )
    return (attn + mixed).astype(jnp.bfloat16)


def shards(
    query,
    keys,
    values,
    lengths,
    routes,
    gates,
    norm_gain,
    old_holds,
    dup_experts,
    w_gate,
    w_up,
    w_down,
):
    width = lax.axis_size("expert")
    features = norm_gain.shape[0]
    expert_list = lax.iota(jnp.int32, old_holds.shape[0])
    holder = jnp.sum(
        expert_list[:, None] * (old_holds[:, None] == expert_list[None, :]).astype(jnp.int32),
        axis=0,
    )
    doubled = jnp.sum((dup_experts[:, None] == expert_list[None, :]).astype(jnp.int32), axis=0)
    own_gate, own_up, own_down = (w_gate[0], w_up[0], w_down[0])
    attn_one = attend(query[0], keys[0], values[0], lengths[0, 0])
    normed_one = normalize(attn_one, norm_gain)
    flat_one, kept_one = routing(routes[0], jnp.ones_like(doubled), holder, holder, 1)
    packed_one, spot_one = pack(normed_one, flat_one, kept_one, (width, CAP // 2, 2))
    received = lax.all_to_all(
        packed_one,
        "expert",
        split_axis=0,
        concat_axis=0,
        tiled=True,
    )
    result = expert_rows(received.reshape(-1, features), own_gate, own_up, own_down)
    back_one = lax.all_to_all(
        result.reshape(received.shape), "expert", split_axis=0, concat_axis=0, tiled=True
    )
    out_one = combine(attn_one, back_one, spot_one, kept_one, gates[0])
    attn_two = attend(query[1], keys[1], values[1], lengths[1, 0])
    normed_two = normalize(attn_two, norm_gain)
    flat_two, kept_two = routing(routes[1], 1 + doubled, holder, holder, 2)
    packed_two, spot_two = gather_pack(normed_two, flat_two, kept_two, (width, CAP, 2))
    received = lax.all_to_all(
        packed_two,
        "expert",
        split_axis=0,
        concat_axis=0,
        tiled=True,
    )
    result = expert_rows(received.reshape(-1, features), own_gate, own_up, own_down).reshape(
        received.shape
    )
    back_two = lax.all_to_all(result, "expert", split_axis=0, concat_axis=0, tiled=True)
    out_two = combine(attn_two, back_two, spot_two, kept_two, gates[1], split=True)
    return jnp.stack([out_one, out_two])


def solution(mesh):
    placed = (
        P(None, ("dp", "expert"), None),
        P(None, ("dp", "expert"), None),
        P(None, ("dp", "expert"), None),
        P(None, ("dp", "expert"), None),
        P(None, ("dp", "expert"), None),
        P(None, ("dp", "expert"), None),
        P(),
        P(),
        P(),
        P("expert", None, None),
        P("expert", None, None),
        P("expert", None, None),
    )
    return jax.shard_map(
        shards,
        mesh=mesh,
        in_specs=placed,
        out_specs=P(None, ("dp", "expert"), None),
        check_vma=False,
    )
```

```python
import jax
import jax.numpy as jnp
from jax import lax
from jax.sharding import PartitionSpec as P

HEAD_WIDTH = 128
CAP = 6


def attend(query, key_rows, value_rows, lengths):
    rows = query.shape[0]
    kv_heads = key_rows.shape[1] // HEAD_WIDTH
    query_group = query.shape[1] // HEAD_WIDTH // kv_heads
    ends = jnp.cumsum(lengths)
    position = lax.iota(jnp.int32, rows)
    request = jnp.sum((position[:, None] >= ends[None, :]).astype(jnp.int32), axis=1)
    allowed = (request[:, None] == request[None, :]) & (position[None, :] <= position[:, None])
    query_heads = query.reshape(rows, kv_heads, query_group, HEAD_WIDTH)
    key_heads = key_rows.reshape(rows, kv_heads, HEAD_WIDTH)
    value_heads = value_rows.reshape(rows, kv_heads, HEAD_WIDTH)
    router_logits = jnp.einsum(
        "qhgd,khd->hgqk", query_heads, key_heads, preferred_element_type=jnp.float32
    ) * HEAD_WIDTH ** (-0.5)
    router_logits = jnp.where(allowed[None, None], router_logits, -1e30)
    highest = jnp.max(router_logits, axis=-1, keepdims=True)
    weights = jnp.exp(router_logits - highest)
    probs = (weights / jnp.sum(weights, axis=-1, keepdims=True)).astype(jnp.bfloat16)
    mixed = jnp.einsum("hgqk,khd->qhgd", probs, value_heads, preferred_element_type=jnp.float32)
    return mixed.reshape(rows, kv_heads * query_group * HEAD_WIDTH)


def normalize(attn, gain):
    meansq = jnp.mean(attn * attn, axis=-1, keepdims=True)
    return (attn * lax.rsqrt(meansq + 1e-05) * gain).astype(jnp.bfloat16)


def expert_rows(rows, gate_mat, up_mat, down_mat):
    gate_val = jnp.dot(rows, gate_mat, preferred_element_type=jnp.float32)
    up_val = jnp.dot(rows, up_mat, preferred_element_type=jnp.float32)
    hidden = (jax.nn.silu(gate_val) * up_val).astype(jnp.bfloat16)
    return jnp.dot(hidden, down_mat, preferred_element_type=jnp.float32).astype(jnp.bfloat16)


def routing(routes, copies_of, first_target, second_target, regions):
    expert_list = lax.iota(jnp.int32, copies_of.shape[0])
    hit = (routes[:, :, None] == expert_list[None, None, :]).astype(jnp.int32)
    named = jnp.sum(hit, axis=1)
    before = jnp.cumsum(named, axis=0) - named
    place = jnp.sum(hit * before[:, None, :], axis=2)
    limit = jnp.sum(hit * copies_of[None, None, :], axis=2)
    kept = place < limit * CAP
    which = place // CAP
    target = jnp.where(
        which == 0,
        jnp.sum(hit * first_target[None, None, :], axis=2),
        jnp.sum(hit * second_target[None, None, :], axis=2),
    )
    flat = (target * CAP + place % CAP) * regions + which
    return (flat, kept)


def pack(normed, flat, kept, shape):
    slots = shape[0] * shape[1] * shape[2]
    spot = jnp.where(kept, flat, slots)
    hit = spot[None, :, :] == lax.iota(jnp.int32, slots)[:, None, None]
    picker = jnp.any(hit, axis=2).astype(normed.dtype).reshape(shape + (normed.shape[0],))
    packed = jnp.einsum("abct,tf->abcf", picker, normed, preferred_element_type=jnp.float32)
    return (packed.astype(normed.dtype), spot)


def gather_pack(normed, flat, kept, shape):
    slots = shape[0] * shape[1] * shape[2]
    tok_rows = normed.shape[0]
    token = jnp.broadcast_to(lax.iota(jnp.int32, tok_rows)[:, None], flat.shape)
    spot = jnp.where(kept, flat, slots)
    source_row = jnp.full((slots,), tok_rows, jnp.int32).at[spot].set(token, mode="drop")
    padded = jnp.concatenate([normed, jnp.zeros((1, normed.shape[1]), normed.dtype)], axis=0)
    return (padded[source_row].reshape(shape + (normed.shape[1],)), spot)


def combine(attn, returned, spot, kept, gates, precision=lax.Precision.HIGHEST):
    slots = returned.size // returned.shape[-1]
    weight = jnp.where(kept, gates, 0.0)
    onehot = (spot[:, :, None] == lax.iota(jnp.int32, slots)[None, None, :]).astype(jnp.float32)
    spread = jnp.sum(onehot * weight[:, :, None], axis=1).reshape((-1,) + returned.shape[:-1])
    mixed = jnp.einsum(
        "tabc,abcf->tf",
        spread,
        returned.astype(jnp.float32),
        precision=precision,
        preferred_element_type=jnp.float32,
    )
    return (attn + mixed).astype(jnp.bfloat16)


def shards(
    query,
    keys,
    values,
    lengths,
    routes,
    gates,
    norm_gain,
    old_holds,
    dup_experts,
    w_gate,
    w_up,
    w_down,
):
    width = lax.axis_size("expert")
    features = norm_gain.shape[0]
    expert_list = lax.iota(jnp.int32, old_holds.shape[0])
    holder = jnp.sum(
        expert_list[:, None] * (old_holds[:, None] == expert_list[None, :]).astype(jnp.int32),
        axis=0,
    )
    doubled = jnp.sum((dup_experts[:, None] == expert_list[None, :]).astype(jnp.int32), axis=0)
    own_gate, own_up, own_down = (w_gate[0], w_up[0], w_down[0])
    attn_one = attend(query[0], keys[0], values[0], lengths[0, 0])
    normed_one = normalize(attn_one, norm_gain)
    flat_one, kept_one = routing(routes[0], jnp.ones_like(doubled), holder, holder, 1)
    packed_one, spot_one = pack(normed_one, flat_one, kept_one, (width, CAP // 2, 2))
    received = lax.all_to_all(
        packed_one,
        "expert",
        split_axis=0,
        concat_axis=0,
        tiled=True,
    )
    result = expert_rows(received.reshape(-1, features), own_gate, own_up, own_down)
    back_one = lax.all_to_all(
        result.reshape(received.shape), "expert", split_axis=0, concat_axis=0, tiled=True
    )
    out_one = combine(attn_one, back_one, spot_one, kept_one, gates[0])
    attn_two = attend(query[1], keys[1], values[1], lengths[1, 0])
    normed_two = normalize(attn_two, norm_gain)
    flat_two, kept_two = routing(routes[1], 1 + doubled, holder, holder, 2)
    packed_two, spot_two = gather_pack(normed_two, flat_two, kept_two, (width, CAP, 2))
    received = lax.all_to_all(
        packed_two,
        "expert",
        split_axis=0,
        concat_axis=0,
        tiled=True,
    )
    result = expert_rows(received.reshape(-1, features), own_gate, own_up, own_down).reshape(
        received.shape
    )
    back_two = lax.all_to_all(result, "expert", split_axis=0, concat_axis=0, tiled=True)
    out_two = combine(attn_two, back_two, spot_two, kept_two, gates[1], lax.Precision.HIGH)
    return jnp.stack([out_one, out_two])


def solution(mesh):
    placed = (
        P(None, ("dp", "expert"), None),
        P(None, ("dp", "expert"), None),
        P(None, ("dp", "expert"), None),
        P(None, ("dp", "expert"), None),
        P(None, ("dp", "expert"), None),
        P(None, ("dp", "expert"), None),
        P(),
        P(),
        P(),
        P("expert", None, None),
        P("expert", None, None),
        P("expert", None, None),
    )
    return jax.shard_map(
        shards,
        mesh=mesh,
        in_specs=placed,
        out_specs=P(None, ("dp", "expert"), None),
        check_vma=False,
    )
```
